32 devices in a mesh: row: 8 (over z, core), col: 4 (over y, x).
Axes of the slice: x: 2, y: 2, z: 4, core: 2. Of those that a mesh axis runs over, the one named last changes fastest.
Arguments:
- atom_feats: bfloat16 [5120, 128], P(('row', 'col')), may hold values from -6 to 6
- atom_bias: float32 [4, 5120, 128], P(None, ('row', 'col')), may hold values from -5 to 360
- atom_counts: int32 [1280], replicated, may hold values from 1 to 24, 5120 in all
- valid_tokens: int32 [1], replicated, may hold values from 640 to 1280
- pair_in: bfloat16 [256, 1280, 128], P('row', 'col'), may hold values from -6 to 6
- atom_gain: float32 [128], replicated, may hold values from 0.5 to 1.5
- atom_proj: bfloat16 [128, 512], replicated, may hold values from -0.5 to 0.5
- atom_out: bfloat16 [128, 128], replicated, may hold values from -4 to 4
- atom_pool: bfloat16 [128, 384], replicated, may hold values from -0.5 to 0.5
- single_to_pair: bfloat16 [384, 256], replicated, may hold values from -0.3125 to 0.3125
- pair_gains: float32 [3, 128], replicated, may hold values from 0.5 to 1.5
- trans_in: bfloat16 [128, 1024], replicated, may hold values from -0.5 to 0.5
- trans_out: bfloat16 [512, 128], replicated, may hold values from -0.25 to 0.25
- tri_in: bfloat16 [128, 512], replicated, may hold values from -0.5 to 0.5
- tri_out: bfloat16 [128, 128], replicated, may hold values from -0.5 to 0.5
Outputs:
- single: bfloat16 [1280, 384], P('col')
- update: bfloat16 [256, 256, 128], P('row', 'col')
The draws below stay inside these ranges and needn't reach their ends.
Inputs may be any that keep to these rules, and one draw needn't show every extreme that they name: `atom_counts`: the counts sum to 5120; some token has exactly 24 atoms.
All inputs are finite; a program needn't handle non-finite values.
Results may differ from the reference program's by a relative error of at most 0.0091.
Values may be sent and summed in bfloat16 or wider, within the bound.
No kernel may reach another device: no remote copies, remote signals or barrier semaphores. Data moves between devices by JAX's collectives and lax.ppermute only.
A program may use at most 128 MiB of HBM per device.

```python
import math
import jax
import jax.numpy as jnp
import numpy as np
from jax import lax

C = 128
CS = 384
CA = 128
HEADS_A = 4
HEAD_DIM = 32
QBLOCK = 32
KEYS = 128
RIM = 48
MOST = 24
SLAB = 256
TOKENS = 1280
ATOMS = 5120


def draw_atom_bias(key, part):
    array_shape = (HEADS_A, ATOMS, KEYS)
    normal_part = jax.random.normal(key, array_shape, jnp.float32)
    return jnp.clip(normal_part, -5.0, 5.0)


def steps_of(key, shape, cuts, least, high):
    loudness = 1.0
    for axis_at, shards_of in cuts:
        steps = jax.random.uniform(jax.random.fold_in(jax.random.fold_in(key, 6), axis_at), (shards_of,), jnp.float32, least / len(cuts), high / len(cuts))
        loudness = loudness * jnp.repeat(jnp.exp(steps), shape[axis_at] // shards_of).reshape((-1,) + (1,) * (len(shape) - 1 - axis_at))
    return loudness


def length_profile(count, total, reach, slope):
    weights = [(1 << 20) // math.isqrt(rank ** slope) + 1 for rank in range(2, count + 1)]
    rest, counts = total - reach - (count - 1), [1] * (count - 1)
    while rest > 0:
        free = [i for i in range(count - 1) if counts[i] < reach]
        mass, budget = sum([weights[i] for i in free]), rest
        for i in free:
            more = min(reach - counts[i], max(1, budget * weights[i] // mass), rest)
            counts[i] = counts[i] + more
            rest = rest - more
    return np.array([reach] + counts)


def uneven(rng, number_of, total, most, slope):
    if number_of == 2:
        one = jax.random.randint(rng, (), max(1, total - most), min(most, total - 1) + 1)
        return jnp.stack([one, total - one])
    tallies = jnp.asarray(length_profile(number_of, total, most, slope), jnp.int32)
    twos = (number_of - 1) // 2
    source_of, taker = tallies[1:1 + 2 * twos:2], tallies[2:2 + 2 * twos:2]
    margin = jnp.minimum(source_of - 1, most - taker)
    moved = jax.random.randint(jax.random.fold_in(rng, 1), (twos,), 0, 1 << 20) % (margin + 1)
    tallies = tallies.at[1:1 + 2 * twos:2].set(source_of - moved).at[2:2 + 2 * twos:2].set(taker + moved)
    return tallies[jax.random.permutation(jax.random.fold_in(rng, 2), number_of)]


def noise(own_key, shape, width, reach, cuts=(), kind=jnp.bfloat16):
    entries = width * jax.random.normal(own_key, shape, jnp.float32)
    if cuts:
        entries = entries * steps_of(own_key, shape, cuts, -0.22, 0.18)
    return jnp.clip(entries, -reach, reach).astype(kind)


def setup_inputs(seed: int = 0) -> dict:
    splits = jax.random.split(jax.random.key(seed), 16)
    return {
        "atom_feats": noise(splits[0], (ATOMS, CA), 1.0, 6.0, ((0, 32),)),
        "atom_bias": draw_atom_bias(jax.random.fold_in(splits[15], 71), 0),
        "atom_counts": uneven(splits[2], TOKENS, ATOMS, MOST, 2).astype(jnp.int32),
        "valid_tokens": jax.random.randint(splits[3], (1,), TOKENS // 2, TOKENS + 1).astype(jnp.int32),
        "pair_in": noise(splits[4], (SLAB, TOKENS, C), 1.0, 6.0, ((0, 8), (1, 4))),
        "atom_gain": jnp.clip(1.0 + 0.1 * jax.random.normal(splits[5], (CA,), jnp.float32), 0.5, 1.5),
        "atom_proj": noise(splits[6], (CA, 4 * CA), CA ** -0.5, 0.5),
        "atom_out": noise(splits[7], (CA, CA), (CA // 64) ** -0.5, 4.0),
        "atom_pool": noise(splits[8], (CA, CS), CA ** -0.5, 0.5),
        "single_to_pair": noise(splits[9], (CS, 2 * C), CS ** -0.5, 0.3125),
        "pair_gains": jnp.clip(1.0 + 0.1 * jax.random.normal(splits[10], (3, C), jnp.float32), 0.5, 1.5),
        "trans_in": noise(splits[11], (C, 8 * C), C ** -0.5, 0.5),
        "trans_out": noise(splits[12], (4 * C, C), (4 * C) ** -0.5, 0.25),
        "tri_in": noise(splits[13], (C, 4 * C), C ** -0.5, 0.5),
        "tri_out": noise(splits[14], (C, C), C ** -0.5, 0.5),
    }


EPS = 1e-05

def normalize(values, gain_row):
    values = values.astype(jnp.float32)
    average = lax.optimization_barrier(jnp.mean(values, axis=-1, keepdims=True))
    centered = values - average
    variance = lax.optimization_barrier(jnp.mean(centered * centered, axis=-1, keepdims=True))
    return centered * lax.rsqrt(variance + EPS) * gain_row

def reference(atom_feats, atom_bias, atom_counts, valid_tokens, pair_in, atom_gain, atom_proj, atom_out, atom_pool, single_to_pair, pair_gains, trans_in, trans_out, tri_in, tri_out):
    normed = normalize(atom_feats, atom_gain).astype(jnp.bfloat16)
    projected = jnp.dot(normed, atom_proj, preferred_element_type=jnp.float32)
    queries = projected[:, :CA].astype(jnp.bfloat16)
    key_vals = projected[:, CA:3 * CA].astype(jnp.bfloat16)
    gating = jax.nn.sigmoid(projected[:, 3 * CA:])
    padded = jnp.pad(key_vals, ((RIM, RIM), (0, 0)))
    blocks = ATOMS // QBLOCK
    indices = (jnp.arange(blocks, dtype=jnp.int32) * QBLOCK)[:, None] + jnp.arange(KEYS, dtype=jnp.int32)[None, :]
    windowed = padded[indices]
    in_range = (indices >= RIM) & (indices < ATOMS + RIM)
    query_heads = queries.reshape(blocks, QBLOCK, HEADS_A, HEAD_DIM).astype(jnp.float32)
    key_heads = windowed[:, :, :CA].reshape(blocks, KEYS, HEADS_A, HEAD_DIM).astype(jnp.float32)
    value_heads = windowed[:, :, CA:].reshape(blocks, KEYS, HEADS_A, HEAD_DIM).astype(jnp.float32)
    scores = jnp.einsum('bqhd,bkhd->bhqk', query_heads, key_heads) * HEAD_DIM ** (-0.5)
    bias_rows = atom_bias.astype(jnp.float32).reshape(HEADS_A, blocks, QBLOCK, KEYS).transpose(1, 0, 2, 3)
    scores = jnp.where(in_range[:, None, None, :], scores + bias_rows, -1e+30)
    row_max = lax.optimization_barrier(jnp.max(scores, axis=-1, keepdims=True))
    exponent = jnp.exp(scores - row_max)
    weights = (exponent / lax.optimization_barrier(jnp.sum(exponent, axis=-1, keepdims=True))).astype(jnp.bfloat16)
    blended = jnp.einsum('bhqk,bkhd->bqhd', weights.astype(jnp.float32), value_heads).reshape(ATOMS, CA)
    gated = (blended * gating).astype(jnp.bfloat16)
    updated = (atom_feats.astype(jnp.float32) + jnp.dot(gated, atom_out, preferred_element_type=jnp.float32)).astype(jnp.bfloat16)
    hidden = jax.nn.relu(jnp.dot(updated, atom_pool, preferred_element_type=jnp.float32))
    owners = jnp.repeat(jnp.arange(TOKENS, dtype=jnp.int32), atom_counts, total_repeat_length=ATOMS)
    totals = jax.ops.segment_sum(hidden, owners, num_segments=TOKENS)
    single = (totals / atom_counts.astype(jnp.float32)[:, None]).astype(jnp.bfloat16)
    terms = jnp.dot(single, single_to_pair, preferred_element_type=jnp.float32)
    row_terms = terms[:SLAB, :C]
    col_terms = terms[:, C:]
    col_mask = (jnp.arange(TOKENS, dtype=jnp.int32) < valid_tokens[0]).astype(jnp.float32)[:, None]

    def pair_row(operands):
        row_in, row_add = operands
        paired = (row_in.astype(jnp.float32) + row_add[None, :] + col_terms).astype(jnp.bfloat16)
        normed_row = normalize(paired, pair_gains[0]).astype(jnp.bfloat16)
        gate_up = jnp.dot(normed_row, trans_in, preferred_element_type=jnp.float32)
        inner = (jax.nn.silu(gate_up[:, :4 * C]) * gate_up[:, 4 * C:]).astype(jnp.bfloat16)
        paired = (paired.astype(jnp.float32) + jnp.dot(inner, trans_out, preferred_element_type=jnp.float32)).astype(jnp.bfloat16)
        normed_row = normalize(paired, pair_gains[1]).astype(jnp.bfloat16)
        tri_proj = jnp.dot(normed_row, tri_in, preferred_element_type=jnp.float32)
        left_ops = (jax.nn.sigmoid(tri_proj[:, :C]) * tri_proj[:, C:2 * C] * col_mask).astype(jnp.bfloat16)
        right_ops = (jax.nn.sigmoid(tri_proj[:, 2 * C:3 * C]) * tri_proj[:, 3 * C:] * col_mask).astype(jnp.bfloat16)
        return (left_ops, right_ops)
    left_ops, right_ops = lax.map(pair_row, (pair_in, row_terms))
    summed = jnp.einsum('ikc,jkc->ijc', left_ops.astype(jnp.float32), right_ops.astype(jnp.float32), precision=lax.Precision.HIGHEST)
    normed_out = normalize(summed, pair_gains[2]).astype(jnp.bfloat16)
    update = jnp.dot(normed_out.reshape(SLAB * SLAB, C), tri_out, preferred_element_type=jnp.float32)
    update = update.reshape(SLAB, SLAB, C).astype(jnp.bfloat16)
    return (single, update)
```

```python
import functools

import jax
import jax.numpy as jnp
from jax import lax
from jax.experimental import pallas as pl
from jax.experimental.pallas import tpu as pltpu
from jax.sharding import PartitionSpec as P

QBLOCK = 32
KEYS = 128
RIM = 48
EPS = 1e-05
BF = jnp.bfloat16
F32 = jnp.float32

VMEM = pl.BlockSpec(memory_space=pltpu.VMEM)
SMEM = pl.BlockSpec(memory_space=pltpu.SMEM)
NT = (((1,), (1,)), ((), ()))
TN = (((0,), (0,)), ((), ()))


def params(limit=48):
    return pltpu.CompilerParams(vmem_limit_bytes=limit << 20)


def cost(flops, nbytes):
    return pl.CostEstimate(flops=int(flops), bytes_accessed=int(nbytes), transcendentals=0)


def dot(a, b, dims=(((1,), (0,)), ((), ()))):
    return lax.dot_general(a, b, dims, preferred_element_type=F32)


def normalize(values, gain, axis):
    average = jnp.mean(values, axis=axis, keepdims=True)
    centered = values - average
    variance = jnp.mean(centered * centered, axis=axis, keepdims=True)
    return centered * lax.rsqrt(variance + EPS) * gain


def atom_kernel(heads, info, before, own, after, gain, proj, bias, out_proj, out, feats):
    rows, width = own.shape
    first, total = info[0], info[1]
    feats[0:RIM, :] = before[...]
    feats[RIM : RIM + rows, :] = own[...]
    feats[RIM + rows :, :] = after[...]
    normed = normalize(feats[...].astype(F32), gain[...], -1).astype(BF)
    projected = dot(normed, proj[...])
    queries = projected[RIM : RIM + rows, :width].astype(BF)
    keys = projected[:, width : 2 * width].astype(BF)
    values = projected[:, 2 * width : 3 * width].astype(BF)
    gating = 0.5 + 0.5 * jnp.tanh(0.5 * projected[RIM : RIM + rows, 3 * width :])
    size = width // heads
    head_of = lax.broadcasted_iota(jnp.int32, (QBLOCK, width), 1) // size
    for b in range(rows // QBLOCK):
        lo = QBLOCK * b
        query = queries[lo : lo + QBLOCK].astype(F32)
        stacked = jnp.concatenate(
            [jnp.where(head_of == h, query, 0.0) for h in range(heads)], axis=0
        ).astype(BF)
        scores = dot(stacked, keys[lo : lo + KEYS], NT) * size ** (-0.5)
        scores = scores + jnp.concatenate([bias[h, lo : lo + QBLOCK, :] for h in range(heads)], axis=0)
        slot = lax.broadcasted_iota(jnp.int32, scores.shape, 1) + (first - RIM + lo)
        scores = jnp.where((slot >= 0) & (slot < total), scores, -1e30)
        exponent = jnp.exp(scores - jnp.max(scores, axis=-1, keepdims=True))
        weights = (exponent / jnp.sum(exponent, axis=-1, keepdims=True)).astype(BF)
        mixed = dot(weights, values[lo : lo + KEYS])
        blended = jnp.zeros((QBLOCK, width), F32)
        for h in range(heads):
            blended = jnp.where(head_of == h, mixed[QBLOCK * h : QBLOCK * (h + 1)], blended)
        gated = (blended * gating[lo : lo + QBLOCK]).astype(BF)
        own_rows = own[lo : lo + QBLOCK, :].astype(F32)
        out[lo : lo + QBLOCK, :] = (own_rows + dot(gated, out_proj[...])).astype(BF)


CHUNK = 256


def pool_kernel(
    groups, cols, slab, kz, info, starts, *refs
):
    parts, refs = refs[:groups], refs[groups:]
    other, table_row, table_col, pool, to_pair, single, row_terms, col_terms, atoms, sums = refs
    z, core, col = info[0], info[1], info[2]
    rows = parts[0].shape[0] // cols
    total = rows * cols * 2 * groups
    for d in range(groups):
        zz = lax.rem(z - d + groups, groups)
        for c in range(cols):
            for s in range(2):
                place = (zz * 2 + (core if s == 0 else 1 - core)) * cols + jnp.bitwise_xor(col, c)
                source = (
                    parts[d][rows * c : rows * (c + 1), :]
                    if s == 0
                    else other[rows * (d * cols + c) : rows * (d * cols + c + 1), :]
                )
                atoms[pl.ds(pl.multiple_of(place * rows, 32), rows), :] = source
    atoms[total:, :] = jnp.zeros((atoms.shape[0] - total, atoms.shape[1]), BF)

    def block(table, lo, count, first_token):
        begin = starts[first_token]
        finish = starts[first_token + count]
        opens = table[lo : lo + count, 0:1]
        closes = table[lo : lo + count, 1:2]
        first = lax.div(begin, CHUNK)
        last = lax.div(finish + CHUNK - 1, CHUNK)

        sums[0:count, :] = jnp.zeros((count, sums.shape[1]), F32)

        def step(i, carry):
            base = pl.multiple_of(i * CHUNK, CHUNK)
            hidden = jnp.maximum(dot(atoms[pl.ds(base, CHUNK), :], pool[...]), 0.0)
            high = hidden.astype(BF)
            low = (hidden - high.astype(F32)).astype(BF)
            place = lax.broadcasted_iota(jnp.int32, (count, CHUNK), 1) + base
            hot = jnp.where((place >= opens) & (place < closes), 1.0, 0.0).astype(BF)
            sums[0:count, :] += dot(hot, high) + dot(hot, low)
            return carry

        lax.fori_loop(first, last, step, 0)
        return (sums[0:count, :] / (closes - opens).astype(F32)).astype(BF)

    tokens = single.shape[0]
    half = tokens // 2
    for t in range(2):
        single[half * t : half * (t + 1), :] = block(table_col, half * t, half, col * tokens + half * t)
    width = row_terms.shape[1]
    count = 128
    for t in range(slab // count):
        term = dot(block(table_row, count * t, count, count * t), to_pair[:, :width])
        for u in range(count // 64):
            zz = t * (count // 64) + u
            row_terms[32 * zz : 32 * zz + 32, :] = jnp.where(
                core == 0, term[64 * u : 64 * u + 32], term[64 * u + 32 : 64 * u + 64]
            )
    all_terms = dot(single[...], to_pair[:, width:])
    sums[0:tokens, 0:width] = all_terms
    col_terms[...] = sums[pl.ds(pl.multiple_of(z * kz, 8), kz), 0:width]


def pair_kernel(groups, cols, chunk_at, info, *refs):
    xs, refs = refs[:groups], refs[groups:]
    row_terms, col_terms, gain_in, gain_out, w_in, w_out, w_tri, eye = refs[:8]
    lefts, rights = refs[8 : 8 + cols], refs[8 + cols : 8 + 2 * cols]
    rows_buf, left_buf, right_buf = refs[8 + 2 * cols :]
    z, k_first, valid = info[0], info[1], info[2]
    kb, per, channels = xs[0].shape
    lanes = per * groups
    for d in range(groups):
        zz = lax.rem(z - d + groups, groups)
        rows_buf[:, pl.ds(pl.multiple_of(zz * per, 32), per), :] = xs[d][...]
    at = k_first + chunk_at + pl.program_id(0) * kb
    tile = max(1, 256 // lanes)
    hidden = w_in.shape[0] // 2
    for t in range(0, kb, tile):
        added = [
            (
                rows_buf[t + u].astype(F32) + row_terms[...] + col_terms[t + u : t + u + 1, :]
            ).astype(BF)
            for u in range(tile)
        ]
        paired = dot(eye[...], jnp.concatenate(added, axis=0), NT)
        normed = normalize(paired, gain_in[...], 0).astype(BF)
        gate_up = dot(w_in[...], normed)
        gate = 0.5 * gate_up[:hidden]
        inner = ((gate + gate * jnp.tanh(gate)) * gate_up[hidden:]).astype(BF)
        following = (paired + dot(w_out[...], inner)).astype(BF).astype(F32)
        normed = normalize(following, gain_out[...], 0).astype(BF)
        ops = dot(w_tri[...], normed)
        gate_l = jnp.tanh(0.5 * ops[:channels])
        gate_r = jnp.tanh(0.5 * ops[2 * channels : 3 * channels])
        val_l = ops[channels : 2 * channels]
        val_r = ops[3 * channels :]
        for u in range(tile):
            scale = jnp.where(at + t + u < valid, 0.5, 0.0).astype(F32)
            span = slice(lanes * u, lanes * (u + 1))
            left = val_l[:, span] * scale
            right = val_r[:, span] * scale
            left = left + left * gate_l[:, span]
            right = right + right * gate_r[:, span]
            for w in range(lanes // 128):
                part = slice(128 * w, 128 * (w + 1))
                left_buf[w, pl.ds(t + u, channels, stride=kb), :] = left[:, part]
                right_buf[w, pl.ds(t + u, channels, stride=kb), :] = right[:, part]
    each = channels // cols
    for d in range(cols):
        for w in range(lanes // 128):
            part = slice(128 * w, 128 * (w + 1))
            span = slice(each * kb * d, each * kb * (d + 1))
            lefts[d][:, :, part] = left_buf[w, span, :].reshape(each, kb, 128).astype(BF)
            rights[d][:, :, part] = right_buf[w, span, :].reshape(each, kb, 128).astype(BF)


CGROUP = 16


def triangle_kernel(groups, count, info, *refs):
    lefts, own, other = refs[:count], refs[count : 2 * count], refs[2 * count : 3 * count]
    outs, buf = refs[3 * count : 3 * count + groups], refs[-1]
    z = info[0]
    lanes = lefts[0].shape[2]
    for c in range(CGROUP):
        left = jnp.concatenate([ref[c] for ref in lefts], axis=0)
        for s, side in enumerate((own, other)):
            right = jnp.concatenate([ref[c] for ref in side], axis=0)
            total = dot(left, right, TN)
            for w in range(lanes // 128):
                buf[s * (lanes // 128) + w, pl.ds(c, lanes, stride=CGROUP), :] = total[
                    :, 128 * w : 128 * (w + 1)
                ]
    for d in range(groups):
        zz = lax.rem(z + d, groups)
        for w in range(2 * lanes // 128):
            piece = buf[w, pl.ds(pl.multiple_of(zz * 32 * CGROUP, 32), 32 * CGROUP), :]
            outs[d][:, :, 128 * w : 128 * (w + 1)] = piece.reshape(32, CGROUP, 128).astype(BF)


def gather_kernel(groups, cols, *refs):
    parts, out = refs[:groups], refs[groups]
    total = parts[0][...].astype(F32)
    for d in range(1, groups):
        total = total + parts[d][...].astype(F32)
    half = total.shape[2] // 2
    split = total.shape[0] // 2
    for col in range(cols):
        pieces = [
            total[split * r : split * (r + 1), :, half * s + 32 * col : half * s + 32 * (col + 1)]
            for r in range(2)
            for s in range(2)
        ]
        out[col] = jnp.concatenate(pieces, axis=-1).astype(BF)


def finish_kernel(cols, info, summed, gain, w_out, update):
    core = info[1]
    split = summed.shape[1]
    for r in range(split):
        values = jnp.concatenate([summed[c, r] for c in range(cols)], axis=0).astype(F32)
        normed = normalize(values, gain[...], 0).astype(BF)
        rows = dot(normed, w_out[...], TN).astype(BF)
        for p in range(2):
            for s in range(2):
                at = pl.multiple_of((core if s == 0 else 1 - core) * 32, 32)
                update[split * p + r, pl.ds(at, 32), :] = rows[64 * p + 32 * s : 64 * p + 32 * s + 32]


def body(
    atom_feats,
    atom_bias,
    atom_counts,
    valid_tokens,
    pair_in,
    atom_gain,
    atom_proj,
    atom_out,
    atom_pool,
    single_to_pair,
    pair_gains,
    trans_in,
    trans_out,
    tri_in,
    tri_out,
):
    atom_rows, atom_width = atom_feats.shape
    rows_n, cols = lax.axis_size("row"), lax.axis_size("col")
    groups = rows_n // 2
    row, col = lax.axis_index("row"), lax.axis_index("col")
    z, core = row // 2, row % 2
    position = row * cols + col
    total_atoms = atom_rows * rows_n * cols
    tokens = atom_counts.shape[0]
    row_dev, tok_col, channels = pair_in.shape
    slab = row_dev * rows_n
    kz = tok_col // groups
    lanes = row_dev * groups
    each = channels // cols
    i32 = jnp.int32

    size = rows_n * cols
    up = [(i, i + 1) for i in range(size - 1)]
    down = [(j, i) for i, j in up]
    before = lax.ppermute(atom_feats[atom_rows - RIM :], ("row", "col"), up)
    after = lax.ppermute(atom_feats[:RIM], ("row", "col"), down)

    def shift_z(value, d):
        pairs = [(i, (i + 2 * d) % rows_n) for i in range(rows_n)]
        return lax.ppermute(value, "row", pairs)

    def cross_col(value, d):
        return lax.ppermute(value, "col", [(i, i ^ d) for i in range(cols)])

    def swap_core(value):
        return lax.ppermute(value, "row", [(i, i ^ 1) for i in range(rows_n)])

    turned = pair_in.transpose(1, 0, 2)
    pair_parts = []
    for d in range(groups):
        share = lax.dynamic_slice_in_dim(turned, ((z + d) % groups) * kz, kz, 0)
        pair_parts.append(shift_z(share, d) if d else share)

    heads = atom_bias.shape[0]
    updated = pl.pallas_call(
        functools.partial(atom_kernel, heads),
        out_shape=jax.ShapeDtypeStruct((atom_rows, atom_width), BF),
        in_specs=[SMEM] + [VMEM] * 7,
        out_specs=VMEM,
        scratch_shapes=[pltpu.VMEM((atom_rows + 2 * RIM, atom_width), BF)],
        compiler_params=params(),
        cost_estimate=cost(1e8, 1e6),
        name="atoms",
    )(
        jnp.stack([position * atom_rows, jnp.asarray(total_atoms, i32)]).astype(i32),
        before,
        atom_feats,
        after,
        atom_gain[None, :],
        atom_proj,
        atom_bias,
        atom_out,
    )

    plane = jnp.concatenate([updated] + [cross_col(updated, d) for d in range(1, cols)], axis=0)
    planes = [plane] + [shift_z(plane, d) for d in range(1, groups)]
    other = swap_core(jnp.concatenate(planes, axis=0))

    ends = jnp.cumsum(atom_counts)
    starts = ends - atom_counts
    table = jnp.stack([starts, ends], axis=1)
    starts_all = jnp.concatenate([jnp.zeros((1,), i32), ends]).astype(i32)
    info = jnp.stack([z, core, col]).astype(i32)
    width = atom_pool.shape[1]
    padded_atoms = -(-total_atoms // CHUNK) * CHUNK + 32
    single, row_terms, col_terms = pl.pallas_call(
        functools.partial(pool_kernel, groups, cols, slab, kz),
        out_shape=(
            jax.ShapeDtypeStruct((tok_col, width), BF),
            jax.ShapeDtypeStruct((lanes, channels), F32),
            jax.ShapeDtypeStruct((kz, channels), F32),
        ),
        in_specs=[SMEM, SMEM] + [VMEM] * (groups + 5),
        out_specs=(VMEM, VMEM, VMEM),
        scratch_shapes=[
            pltpu.VMEM((padded_atoms, atom_width), BF),
            pltpu.VMEM((tok_col, width), F32),
        ],
        compiler_params=params(),
        cost_estimate=cost(1e9, 4e6),
        name="pool",
    )(
        info,
        starts_all,
        *planes,
        other,
        table[:slab],
        lax.dynamic_slice_in_dim(table, col * tok_col, tok_col),
        atom_pool,
        single_to_pair,
    )

    order = jnp.bitwise_xor(col, jnp.arange(cols, dtype=i32))
    w_tri = tri_in.T.reshape(4, cols, each, channels)
    w_tri = jnp.take(w_tri, order, axis=1).reshape(4 * channels, channels)
    unit = kz // 5
    tile_lanes = max(256, lanes)
    gain_in = jnp.broadcast_to(pair_gains[0][:, None], (channels, tile_lanes))
    gain_out = jnp.broadcast_to(pair_gains[1][:, None], (channels, tile_lanes))
    pair_info = jnp.stack([z, col * tok_col + z * kz, valid_tokens[0]]).astype(i32)
    eye = jnp.eye(channels, dtype=BF)
    lefts, rights = [], []
    at = 0
    for steps in (1, 2, 2):
        first = at
        whole = lambda *shape: pl.BlockSpec(shape, lambda g: (0,) * len(shape))
        outs = pl.pallas_call(
            functools.partial(pair_kernel, groups, cols, first * unit),
            grid=(steps,),
            out_shape=[jax.ShapeDtypeStruct((each, steps * unit, lanes), BF)] * (2 * cols),
            in_specs=[SMEM]
            + [pl.BlockSpec((unit, row_dev, channels), lambda g, first=first: (first + g, 0, 0))]
            * groups
            + [
                whole(lanes, channels),
                pl.BlockSpec((unit, channels), lambda g, first=first: (first + g, 0)),
                whole(channels, tile_lanes),
                whole(channels, tile_lanes),
                whole(*trans_in.shape[::-1]),
                whole(*trans_out.shape[::-1]),
                whole(4 * channels, channels),
                whole(channels, channels),
            ],
            out_specs=[pl.BlockSpec((each, unit, lanes), lambda g: (0, g, 0))] * (2 * cols),
            scratch_shapes=[
                pltpu.VMEM((unit, lanes, channels), BF),
                pltpu.VMEM((lanes // 128, channels * unit, 128), F32),
                pltpu.VMEM((lanes // 128, channels * unit, 128), F32),
            ],
            compiler_params=params(),
            cost_estimate=cost(steps * unit * lanes * 524288, steps * unit * lanes * channels * 6),
            name="pair",
        )(
            pair_info,
            *pair_parts,
            row_terms,
            col_terms,
            gain_in,
            gain_out,
            trans_in.T,
            trans_out.T,
            w_tri,
            eye,
        )
        at += steps
        for d in range(cols):
            left, right = outs[d], outs[cols + d]
            lefts.append(cross_col(left, d) if d else left)
            rights.append(cross_col(right, d) if d else right)
    others = [swap_core(right) for right in rights]

    count = len(lefts)
    specs = [pl.BlockSpec((CGROUP,) + v.shape[1:], lambda g: (g, 0, 0)) for v in lefts]
    sent = pl.pallas_call(
        functools.partial(triangle_kernel, groups, count),
        grid=(each // CGROUP,),
        out_shape=[jax.ShapeDtypeStruct((row_dev, each, 2 * lanes), BF)] * groups,
        in_specs=[SMEM] + specs * 3,
        out_specs=[pl.BlockSpec((row_dev, CGROUP, 2 * lanes), lambda g: (0, g, 0))] * groups,
        scratch_shapes=[pltpu.VMEM((2 * lanes // 128, lanes * CGROUP, 128), F32)],
        compiler_params=params(),
        cost_estimate=cost(2 * each * lanes * 2 * lanes * tok_col, 2e7),
        name="triangle",
    )(info, *lefts, *rights, *others)
    parts = [shift_z(part, d) if d else part for d, part in enumerate(sent)]
    gathered = pl.pallas_call(
        functools.partial(gather_kernel, groups, cols),
        out_shape=jax.ShapeDtypeStruct((cols, row_dev // 2, each, 128), BF),
        in_specs=[VMEM] * groups,
        out_specs=VMEM,
        compiler_params=params(),
        cost_estimate=cost(1e6, 3e6),
        name="gather",
    )(*parts)
    summed = lax.all_to_all(gathered, "col", split_axis=0, concat_axis=0, tiled=True)
    update = pl.pallas_call(
        functools.partial(finish_kernel, cols),
        out_shape=jax.ShapeDtypeStruct((row_dev, slab // cols, channels), BF),
        in_specs=[SMEM] + [VMEM] * 3,
        out_specs=VMEM,
        compiler_params=params(),
        cost_estimate=cost(1e8, 1e6),
        name="finish",
    )(info, summed, jnp.broadcast_to(pair_gains[2][:, None], (channels, 128)), tri_out)
    return (single, update)


def solution(mesh):
    in_specs = (
        P(("row", "col"), None),
        P(None, ("row", "col"), None),
        P(),
        P(),
        P("row", "col", None),
        P(),
        P(),
        P(),
        P(),
        P(),
        P(),
        P(),
        P(),
        P(),
        P(),
    )
    out_specs = (P("col", None), P("row", "col", None))
    return jax.shard_map(body, mesh=mesh, in_specs=in_specs, out_specs=out_specs, check_vma=False)
```

```python
import functools

import jax
import jax.numpy as jnp
from jax import lax
from jax.experimental import pallas as pl
from jax.experimental.pallas import tpu as pltpu
from jax.sharding import PartitionSpec as P

QBLOCK = 32
KEYS = 128
RIM = 48
EPS = 1e-05
BF = jnp.bfloat16
F32 = jnp.float32

VMEM = pl.BlockSpec(memory_space=pltpu.VMEM)
SMEM = pl.BlockSpec(memory_space=pltpu.SMEM)
NT = (((1,), (1,)), ((), ()))
TN = (((0,), (0,)), ((), ()))


def params(limit=48):
    return pltpu.CompilerParams(vmem_limit_bytes=limit << 20)


def cost(flops, nbytes):
    return pl.CostEstimate(flops=int(flops), bytes_accessed=int(nbytes), transcendentals=0)


def dot(a, b, dims=(((1,), (0,)), ((), ()))):
    return lax.dot_general(a, b, dims, preferred_element_type=F32)


def normalize(values, gain, axis):
    average = jnp.mean(values, axis=axis, keepdims=True)
    centered = values - average
    variance = jnp.mean(centered * centered, axis=axis, keepdims=True)
    return centered * lax.rsqrt(variance + EPS) * gain


def atom_kernel(heads, info, before, own, after, gain, proj, bias, out_proj, out, feats):
    rows, width = own.shape
    first, total = info[0], info[1]
    feats[0:RIM, :] = before[...]
    feats[RIM : RIM + rows, :] = own[...]
    feats[RIM + rows :, :] = after[...]
    normed = normalize(feats[...].astype(F32), gain[...], -1).astype(BF)
    projected = dot(normed, proj[...])
    queries = projected[RIM : RIM + rows, :width].astype(BF)
    keys = projected[:, width : 2 * width].astype(BF)
    values = projected[:, 2 * width : 3 * width].astype(BF)
    gating = 0.5 + 0.5 * jnp.tanh(0.5 * projected[RIM : RIM + rows, 3 * width :])
    size = width // heads
    head_of = lax.broadcasted_iota(jnp.int32, (QBLOCK, width), 1) // size
    for b in range(rows // QBLOCK):
        lo = QBLOCK * b
        query = queries[lo : lo + QBLOCK].astype(F32)
        stacked = jnp.concatenate(
            [jnp.where(head_of == h, query, 0.0) for h in range(heads)], axis=0
        ).astype(BF)
        scores = dot(stacked, keys[lo : lo + KEYS], NT) * size ** (-0.5)
        scores = scores + jnp.concatenate([bias[h, lo : lo + QBLOCK, :] for h in range(heads)], axis=0)
        slot = lax.broadcasted_iota(jnp.int32, scores.shape, 1) + (first - RIM + lo)
        scores = jnp.where((slot >= 0) & (slot < total), scores, -1e30)
        exponent = jnp.exp(scores - jnp.max(scores, axis=-1, keepdims=True))
        weights = (exponent / jnp.sum(exponent, axis=-1, keepdims=True)).astype(BF)
        mixed = dot(weights, values[lo : lo + KEYS])
        blended = jnp.zeros((QBLOCK, width), F32)
        for h in range(heads):
            blended = jnp.where(head_of == h, mixed[QBLOCK * h : QBLOCK * (h + 1)], blended)
        gated = (blended * gating[lo : lo + QBLOCK]).astype(BF)
        own_rows = own[lo : lo + QBLOCK, :].astype(F32)
        out[lo : lo + QBLOCK, :] = (own_rows + dot(gated, out_proj[...])).astype(BF)


CHUNK = 256


def pool_kernel(
    groups, cols, slab, kz, info, starts, *refs
):
    parts, refs = refs[:groups], refs[groups:]
    other, table_row, table_col, pool, to_pair, single, row_terms, col_terms, atoms, sums = refs
    z, core, col = info[0], info[1], info[2]
    rows = parts[0].shape[0] // cols
    total = rows * cols * 2 * groups
    for d in range(groups):
        zz = lax.rem(z - d + groups, groups)
        for c in range(cols):
            for s in range(2):
                place = (zz * 2 + (core if s == 0 else 1 - core)) * cols + jnp.bitwise_xor(col, c)
                source = (
                    parts[d][rows * c : rows * (c + 1), :]
                    if s == 0
                    else other[rows * (d * cols + c) : rows * (d * cols + c + 1), :]
                )
                atoms[pl.ds(pl.multiple_of(place * rows, 32), rows), :] = source
    atoms[total:, :] = jnp.zeros((atoms.shape[0] - total, atoms.shape[1]), BF)

    def block(table, lo, count, first_token):
        begin = starts[first_token]
        finish = starts[first_token + count]
        opens = table[lo : lo + count, 0:1]
        closes = table[lo : lo + count, 1:2]
        first = lax.div(begin, CHUNK)
        last = lax.div(finish + CHUNK - 1, CHUNK)

        sums[0:count, :] = jnp.zeros((count, sums.shape[1]), F32)

        def step(i, carry):
            base = pl.multiple_of(i * CHUNK, CHUNK)
            hidden = jnp.maximum(dot(atoms[pl.ds(base, CHUNK), :], pool[...]), 0.0)
            high = hidden.astype(BF)
            low = (hidden - high.astype(F32)).astype(BF)
            place = lax.broadcasted_iota(jnp.int32, (count, CHUNK), 1) + base
            hot = jnp.where((place >= opens) & (place < closes), 1.0, 0.0).astype(BF)
            sums[0:count, :] += dot(hot, high) + dot(hot, low)
            return carry

        lax.fori_loop(first, last, step, 0)
        return (sums[0:count, :] / (closes - opens).astype(F32)).astype(BF)

    tokens = single.shape[0]
    half = tokens // 2
    for t in range(2):
        single[half * t : half * (t + 1), :] = block(table_col, half * t, half, col * tokens + half * t)
    width = row_terms.shape[1]
    count = 128
    for t in range(slab // count):
        term = dot(block(table_row, count * t, count, count * t), to_pair[:, :width])
        for u in range(count // 64):
            zz = t * (count // 64) + u
            row_terms[32 * zz : 32 * zz + 32, :] = jnp.where(
                core == 0, term[64 * u : 64 * u + 32], term[64 * u + 32 : 64 * u + 64]
            )
    all_terms = dot(single[...], to_pair[:, width:])
    sums[0:tokens, 0:width] = all_terms
    col_terms[...] = sums[pl.ds(pl.multiple_of(z * kz, 8), kz), 0:width]


def pair_kernel(groups, cols, halves, chunk_at, info, *refs):
    xs, refs = refs[:groups], refs[groups:]
    row_terms, col_terms, gain_in, gain_out, w_in, w_out, w_tri, eye = refs[:8]
    outs, (left_buf, right_buf, rows_buf) = refs[8:-3], refs[-3:]
    k_first, valid, z, col = info[0], info[1], info[2], info[3]
    kb, per, channels = xs[0].shape
    lanes = per * groups
    for d in range(groups):
        zz = lax.rem(z - d + groups, groups)
        rows_buf[:, pl.ds(pl.multiple_of(zz * per, 32), per), :] = xs[d][...]
    at = k_first + chunk_at + pl.program_id(0) * kb
    tile = max(1, 256 // lanes)
    hidden = w_in.shape[0] // 2

    def opening(t):
        added = [
            (
                rows_buf[t + u].astype(F32) + row_terms[...] + col_terms[t + u : t + u + 1, :]
            ).astype(BF)
            for u in range(tile)
        ]
        paired = dot(eye[...], jnp.concatenate(added, axis=0), NT)
        normed = normalize(paired, gain_in[...], 0).astype(BF)
        return paired, dot(w_in[...], normed)

    def closing(t, paired, gate_up):
        gate = 0.5 * gate_up[:hidden]
        inner = ((gate + gate * jnp.tanh(gate)) * gate_up[hidden:]).astype(BF)
        following = (paired + dot(w_out[...], inner)).astype(BF).astype(F32)
        normed = normalize(following, gain_out[...], 0).astype(BF)
        ops = dot(w_tri[...], normed)
        gate_l = jnp.tanh(0.5 * ops[:channels])
        gate_r = jnp.tanh(0.5 * ops[2 * channels : 3 * channels])
        val_l = ops[channels : 2 * channels]
        val_r = ops[3 * channels :]
        for u in range(tile):
            scale = jnp.where(at + t + u < valid, 0.5, 0.0).astype(F32)
            span = slice(lanes * u, lanes * (u + 1))
            left = val_l[:, span] * scale
            right = val_r[:, span] * scale
            left = left + left * gate_l[:, span]
            right = right + right * gate_r[:, span]
            for w in range(lanes // 128):
                part = slice(128 * w, 128 * (w + 1))
                left_buf[w, pl.ds(t + u, channels, stride=kb), :] = left[:, part]
                right_buf[w, pl.ds(t + u, channels, stride=kb), :] = right[:, part]

    ahead = opening(0)
    for t in range(0, kb, tile):
        held = ahead
        if t + tile < kb:
            ahead = opening(t + tile)
        closing(t, *held)
    each = channels // cols
    hc = each // 2
    for d in range(cols):
        for h in range(2):
            if halves == 2 and h == 1:
                out, at = outs[1 + d], (0, 0)
                first = (jnp.bitwise_xor(col, d) * each + hc) * kb
            else:
                out, at = outs[0], (d, h)
                first = (d * each + h * hc) * kb
            span = pl.ds(pl.multiple_of(first, 8), hc * kb)
            for w in range(lanes // 128):
                part = slice(128 * w, 128 * (w + 1))
                for side, buf in enumerate((left_buf, right_buf)):
                    piece = buf[w, span, :].reshape(hc, kb, 128)
                    out[at[0], at[1], side, :, :, part] = piece.astype(BF)


def triangle_kernel(groups, count, info, *refs):
    own, other = refs[:count], refs[count : -groups - 1]
    outs, buf = refs[-groups - 1 : -1], refs[-1]
    z = info[0]
    hc, lanes = own[0].shape[3], own[0].shape[5]
    for c in range(hc):
        left = jnp.concatenate([ref[d, 0, 0, c] for ref in own for d in range(ref.shape[0])], axis=0)
        for s, side in enumerate((own, other)):
            right = jnp.concatenate([ref[d, 0, 1, c] for ref in side for d in range(ref.shape[0])], axis=0)
            total = dot(left, right, TN)
            for w in range(lanes // 128):
                buf[s * (lanes // 128) + w, pl.ds(c, lanes, stride=hc), :] = total[
                    :, 128 * w : 128 * (w + 1)
                ]
    for d in range(groups):
        zz = lax.rem(z + d, groups)
        for w in range(2 * lanes // 128):
            piece = buf[w, pl.ds(pl.multiple_of(zz * 32 * hc, 32), 32 * hc), :]
            outs[d][:, :, 128 * w : 128 * (w + 1)] = piece.reshape(32, hc, 128).astype(BF)


def gather_kernel(groups, cols, *refs):
    parts, out = refs[:groups], refs[groups]
    total = parts[0][...].astype(F32)
    for d in range(1, groups):
        total = total + parts[d][...].astype(F32)
    half = total.shape[2] // 2
    split = total.shape[0] // 2
    for col in range(cols):
        pieces = [
            total[split * r : split * (r + 1), :, half * s + 32 * col : half * s + 32 * (col + 1)]
            for r in range(2)
            for s in range(2)
        ]
        out[col] = jnp.concatenate(pieces, axis=-1).astype(BF)


def finish_kernel(cols, info, first, second, gain, w_out, update):
    core = info[1]
    split = first.shape[1]
    for r in range(split):
        values = jnp.concatenate(
            [half[c, r].astype(F32) for c in range(cols) for half in (first, second)], axis=0
        )
        normed = normalize(values, gain[...], 0).astype(BF)
        rows = dot(normed, w_out[...], TN).astype(BF)
        for p in range(2):
            for s in range(2):
                at = pl.multiple_of((core if s == 0 else 1 - core) * 32, 32)
                update[split * p + r, pl.ds(at, 32), :] = rows[64 * p + 32 * s : 64 * p + 32 * s + 32]


def body(
    atom_feats,
    atom_bias,
    atom_counts,
    valid_tokens,
    pair_in,
    atom_gain,
    atom_proj,
    atom_out,
    atom_pool,
    single_to_pair,
    pair_gains,
    trans_in,
    trans_out,
    tri_in,
    tri_out,
):
    atom_rows, atom_width = atom_feats.shape
    rows_n, cols = lax.axis_size("row"), lax.axis_size("col")
    groups = rows_n // 2
    row, col = lax.axis_index("row"), lax.axis_index("col")
    z, core = row // 2, row % 2
    position = row * cols + col
    total_atoms = atom_rows * rows_n * cols
    tokens = atom_counts.shape[0]
    row_dev, tok_col, channels = pair_in.shape
    slab = row_dev * rows_n
    kz = tok_col // groups
    lanes = row_dev * groups
    each = channels // cols
    i32 = jnp.int32

    size = rows_n * cols
    up = [(i, i + 1) for i in range(size - 1)]
    down = [(j, i) for i, j in up]
    before = lax.ppermute(atom_feats[atom_rows - RIM :], ("row", "col"), up)
    after = lax.ppermute(atom_feats[:RIM], ("row", "col"), down)

    def shift_z(value, d):
        pairs = [(i, (i + 2 * d) % rows_n) for i in range(rows_n)]
        return lax.ppermute(value, "row", pairs)

    def cross_col(value, d):
        return lax.ppermute(value, "col", [(i, i ^ d) for i in range(cols)])

    def swap_core(value):
        return lax.ppermute(value, "row", [(i, i ^ 1) for i in range(rows_n)])

    unit = kz // 5
    chunks = ((0, 2), (2, 3))

    def spread_z(pieces):
        return [shift_z(piece, d) if d else piece for d, piece in enumerate(pieces)]

    def spread_col(value):
        return lax.all_to_all(value, "col", split_axis=0, concat_axis=0, tiled=True)

    def shares(z, first, steps):
        pieces = []
        for d in range(groups):
            start = ((z + d) % groups) * kz + first * unit
            piece = lax.dynamic_slice_in_dim(pair_in, start, steps * unit, 1)
            pieces.append(piece.transpose(1, 0, 2))
        return pieces

    pair_parts = [spread_z(shares(z, *chunks[0]))]

    heads = atom_bias.shape[0]
    updated = pl.pallas_call(
        functools.partial(atom_kernel, heads),
        out_shape=jax.ShapeDtypeStruct((atom_rows, atom_width), BF),
        in_specs=[SMEM] + [VMEM] * 7,
        out_specs=VMEM,
        scratch_shapes=[pltpu.VMEM((atom_rows + 2 * RIM, atom_width), BF)],
        compiler_params=params(),
        cost_estimate=cost(1e8, 1e6),
        name="atoms",
    )(
        jnp.stack([position * atom_rows, jnp.asarray(total_atoms, i32)]).astype(i32),
        before,
        atom_feats,
        after,
        atom_gain[None, :],
        atom_proj,
        atom_bias,
        atom_out,
    )

    updated, z_later, trans_in, trans_out, tri_in, gains = lax.optimization_barrier(
        (updated, z, trans_in, trans_out, tri_in, pair_gains)
    )
    plane = jnp.concatenate([updated] + [cross_col(updated, d) for d in range(1, cols)], axis=0)
    plane, pair_parts[0] = lax.optimization_barrier((plane, pair_parts[0]))
    planes = [plane] + [shift_z(plane, d) for d in range(1, groups)]
    later = [shares(z_later, *chunk) for chunk in chunks[1:]]
    tile_lanes = max(256, lanes)
    weights = [
        jnp.broadcast_to(gains[0][:, None], (channels, tile_lanes)),
        jnp.broadcast_to(gains[1][:, None], (channels, tile_lanes)),
        trans_in.T,
        trans_out.T,
        tri_in.T,
        jnp.eye(channels, dtype=BF),
    ]
    planes, later, weights = lax.optimization_barrier((planes, later, weights))
    other = swap_core(jnp.concatenate(planes, axis=0))
    pair_parts += [spread_z(pieces) for pieces in later]

    ends = jnp.cumsum(atom_counts)
    starts = ends - atom_counts
    table = jnp.stack([starts, ends], axis=1)
    starts_all = jnp.concatenate([jnp.zeros((1,), i32), ends]).astype(i32)
    info = jnp.stack([z, core, col]).astype(i32)
    width = atom_pool.shape[1]
    padded_atoms = -(-total_atoms // CHUNK) * CHUNK + 32
    single, row_terms, col_terms = pl.pallas_call(
        functools.partial(pool_kernel, groups, cols, slab, kz),
        out_shape=(
            jax.ShapeDtypeStruct((tok_col, width), BF),
            jax.ShapeDtypeStruct((lanes, channels), F32),
            jax.ShapeDtypeStruct((kz, channels), F32),
        ),
        in_specs=[SMEM, SMEM] + [VMEM] * (groups + 5),
        out_specs=(VMEM, VMEM, VMEM),
        scratch_shapes=[
            pltpu.VMEM((padded_atoms, atom_width), BF),
            pltpu.VMEM((tok_col, width), F32),
        ],
        compiler_params=params(),
        cost_estimate=cost(1e3, 1e3),
        name="pool",
    )(
        info,
        starts_all,
        *planes,
        other,
        table[:slab],
        lax.dynamic_slice_in_dim(table, col * tok_col, tok_col),
        atom_pool,
        single_to_pair,
    )

    pair_info = jnp.stack([col * tok_col + z * kz, valid_tokens[0], z, col]).astype(i32)
    hc = each // 2
    operands = []

    def swap_joined(values):
        return swap_core(jnp.concatenate(values, axis=0) if len(values) > 1 else values[0])


    def exchange(values):
        operands.append([spread_col(values[0])])
        if len(values) > 1:
            got = [cross_col(value, d) if d else value for d, value in enumerate(values[1:])]
            operands.append(got)

    for call, (first, steps) in enumerate(chunks):
        halves = 2 if call == len(chunks) - 1 else 1
        inner = 2 // halves
        counts = [cols] + [1] * cols * (halves - 1)
        parts = pair_parts[call]
        if call:
            exchange(outs)
            _, parts = lax.optimization_barrier((outs, parts))
        whole = lambda *shape: pl.BlockSpec(shape, lambda g: (0,) * len(shape))
        outs = pl.pallas_call(
            functools.partial(pair_kernel, groups, cols, halves, first * unit),
            grid=(steps,),
            out_shape=[
                jax.ShapeDtypeStruct((blocks, inner, 2, hc, steps * unit, lanes), BF)
                for blocks in counts
            ],
            in_specs=[SMEM]
            + [pl.BlockSpec((unit, row_dev, channels), lambda g: (g, 0, 0))] * groups
            + [
                whole(lanes, channels),
                pl.BlockSpec((unit, channels), lambda g, first=first: (first + g, 0)),
                whole(channels, tile_lanes),
                whole(channels, tile_lanes),
                whole(*trans_in.shape[::-1]),
                whole(*trans_out.shape[::-1]),
                whole(4 * channels, channels),
                whole(channels, channels),
            ],
            out_specs=[
                pl.BlockSpec((blocks, inner, 2, hc, unit, lanes), lambda g: (0, 0, 0, 0, g, 0))
                for blocks in counts
            ],
            scratch_shapes=[
                pltpu.VMEM((lanes // 128, channels * unit, 128), F32),
                pltpu.VMEM((lanes // 128, channels * unit, 128), F32),
                pltpu.VMEM((unit, lanes, channels), BF),
            ],
            compiler_params=params(),
            cost_estimate=cost(*((1e3, 1e3) if call == 0 else (3e10, 1e6))),
            name="pair",
        )(
            pair_info,
            *parts,
            row_terms,
            col_terms,
            *weights,
        )
    for at in range(len(operands)):
        operands[at], outs = lax.optimization_barrier((operands[at], outs))
        operands[at] = (operands[at], [swap_joined(operands[at])])
    exchange(outs)
    sent = None

    def finish_sum(parts):
        gathered = pl.pallas_call(
            functools.partial(gather_kernel, groups, cols),
            out_shape=jax.ShapeDtypeStruct((cols, row_dev // 2, hc, 128), BF),
            in_specs=[VMEM] * groups,
            out_specs=VMEM,
            compiler_params=params(),
            cost_estimate=cost(1e6, 3e6),
            name="gather",
        )(*parts)
        return spread_col(gathered)

    summed = []
    last = len(chunks) - 1
    for h in range(2):
        late = operands[last + h]
        if h:
            parts = spread_z(sent)
            late, parts[groups // 2] = lax.optimization_barrier((late, parts[groups // 2]))
            summed.append(finish_sum(parts))
        pairs = operands[:last] + [(late, [swap_joined(late)])]
        own, others = sum([p[0] for p in pairs], []), sum([p[1] for p in pairs], [])
        specs = [
            pl.BlockSpec(
                v.shape[:1] + (1,) + v.shape[2:],
                lambda g, at=h * (v.shape[1] - 1): (0, at, 0, 0, 0, 0),
            )
            for v in own + others
        ]
        sent = pl.pallas_call(
            functools.partial(triangle_kernel, groups, len(own)),
            grid=(1,),
            out_shape=[jax.ShapeDtypeStruct((row_dev, hc, 2 * lanes), BF)] * groups,
            in_specs=[SMEM] + specs,
            out_specs=[pl.BlockSpec((row_dev, hc, 2 * lanes), lambda g: (0, 0, 0))] * groups,
            scratch_shapes=[pltpu.VMEM((2 * lanes // 128, lanes * hc, 128), F32)],
            compiler_params=params(),
            cost_estimate=cost(4 * hc * lanes * lanes * tok_col, 1e7),
            name="triangle",
        )(info, *own, *others)
    summed.append(finish_sum(spread_z(sent)))
    update = pl.pallas_call(
        functools.partial(finish_kernel, cols),
        out_shape=jax.ShapeDtypeStruct((row_dev, slab // cols, channels), BF),
        in_specs=[SMEM] + [VMEM] * 4,
        out_specs=VMEM,
        compiler_params=params(),
        cost_estimate=cost(1e8, 1e6),
        name="finish",
    )(info, *summed, jnp.broadcast_to(gains[2][:, None], (channels, 128)), tri_out)
    return (single, update)


def solution(mesh):
    in_specs = (
        P(("row", "col"), None),
        P(None, ("row", "col"), None),
        P(),
        P(),
        P("row", "col", None),
        P(),
        P(),
        P(),
        P(),
        P(),
        P(),
        P(),
        P(),
        P(),
        P(),
    )
    out_specs = (P("col", None), P("row", "col", None))
    return jax.shard_map(body, mesh=mesh, in_specs=in_specs, out_specs=out_specs, check_vma=False)
```

```python
import functools

import jax
import jax.numpy as jnp
from jax import lax
from jax.experimental import pallas as pl
from jax.experimental.pallas import tpu as pltpu
from jax.sharding import PartitionSpec as P

QBLOCK = 32
KEYS = 128
RIM = 48
EPS = 1e-05
BF = jnp.bfloat16
F32 = jnp.float32

VMEM = pl.BlockSpec(memory_space=pltpu.VMEM)
SMEM = pl.BlockSpec(memory_space=pltpu.SMEM)
NT = (((1,), (1,)), ((), ()))
TN = (((0,), (0,)), ((), ()))


def params(limit=48):
    return pltpu.CompilerParams(vmem_limit_bytes=limit << 20)


def cost(flops, nbytes):
    return pl.CostEstimate(flops=int(flops), bytes_accessed=int(nbytes), transcendentals=0)


def dot(a, b, dims=(((1,), (0,)), ((), ()))):
    return lax.dot_general(a, b, dims, preferred_element_type=F32)


def normalize(values, gain, axis):
    average = jnp.mean(values, axis=axis, keepdims=True)
    centered = values - average
    variance = jnp.mean(centered * centered, axis=axis, keepdims=True)
    return centered * lax.rsqrt(variance + EPS) * gain


def atom_kernel(heads, info, before, own, after, gain, proj, bias, out_proj, out, feats):
    rows, width = own.shape
    first, total = info[0], info[1]
    feats[0:RIM, :] = before[...]
    feats[RIM : RIM + rows, :] = own[...]
    feats[RIM + rows :, :] = after[...]
    normed = normalize(feats[...].astype(F32), gain[...], -1).astype(BF)
    projected = dot(normed, proj[...])
    queries = projected[RIM : RIM + rows, :width].astype(BF)
    keys = projected[:, width : 2 * width].astype(BF)
    values = projected[:, 2 * width : 3 * width].astype(BF)
    gating = 0.5 + 0.5 * jnp.tanh(0.5 * projected[RIM : RIM + rows, 3 * width :])
    size = width // heads
    head_of = lax.broadcasted_iota(jnp.int32, (QBLOCK, width), 1) // size
    for b in range(rows // QBLOCK):
        lo = QBLOCK * b
        query = queries[lo : lo + QBLOCK].astype(F32)
        stacked = jnp.concatenate(
            [jnp.where(head_of == h, query, 0.0) for h in range(heads)], axis=0
        ).astype(BF)
        scores = dot(stacked, keys[lo : lo + KEYS], NT) * size ** (-0.5)
        scores = scores + jnp.concatenate([bias[h, lo : lo + QBLOCK, :] for h in range(heads)], axis=0)
        slot = lax.broadcasted_iota(jnp.int32, scores.shape, 1) + (first - RIM + lo)
        scores = jnp.where((slot >= 0) & (slot < total), scores, -1e30)
        exponent = jnp.exp(scores - jnp.max(scores, axis=-1, keepdims=True))
        weights = (exponent / jnp.sum(exponent, axis=-1, keepdims=True)).astype(BF)
        mixed = dot(weights, values[lo : lo + KEYS])
        blended = jnp.zeros((QBLOCK, width), F32)
        for h in range(heads):
            blended = jnp.where(head_of == h, mixed[QBLOCK * h : QBLOCK * (h + 1)], blended)
        gated = (blended * gating[lo : lo + QBLOCK]).astype(BF)
        own_rows = own[lo : lo + QBLOCK, :].astype(F32)
        out[lo : lo + QBLOCK, :] = (own_rows + dot(gated, out_proj[...])).astype(BF)


CHUNK = 256


def pool_kernel(
    groups, cols, slab, kz, info, starts, *refs
):
    parts, refs = refs[:groups], refs[groups:]
    other, table_row, table_col, pool, to_pair, single, row_terms, col_terms, atoms, sums = refs
    z, core, col = info[0], info[1], info[2]
    rows = parts[0].shape[0] // cols
    total = rows * cols * 2 * groups
    for d in range(groups):
        zz = lax.rem(z - d + groups, groups)
        for c in range(cols):
            for s in range(2):
                place = (zz * 2 + (core if s == 0 else 1 - core)) * cols + jnp.bitwise_xor(col, c)
                source = (
                    parts[d][rows * c : rows * (c + 1), :]
                    if s == 0
                    else other[rows * (d * cols + c) : rows * (d * cols + c + 1), :]
                )
                atoms[pl.ds(pl.multiple_of(place * rows, 32), rows), :] = source
    atoms[total:, :] = jnp.zeros((atoms.shape[0] - total, atoms.shape[1]), BF)

    def block(table, lo, count, first_token):
        begin = starts[first_token]
        finish = starts[first_token + count]
        opens = table[lo : lo + count, 0:1]
        closes = table[lo : lo + count, 1:2]
        first = lax.div(begin, CHUNK)
        last = lax.div(finish + CHUNK - 1, CHUNK)

        sums[0:count, :] = jnp.zeros((count, sums.shape[1]), F32)

        def step(i, carry):
            base = pl.multiple_of(i * CHUNK, CHUNK)
            hidden = jnp.maximum(dot(atoms[pl.ds(base, CHUNK), :], pool[...]), 0.0)
            high = hidden.astype(BF)
            low = (hidden - high.astype(F32)).astype(BF)
            place = lax.broadcasted_iota(jnp.int32, (count, CHUNK), 1) + base
            hot = jnp.where((place >= opens) & (place < closes), 1.0, 0.0).astype(BF)
            sums[0:count, :] += dot(hot, high) + dot(hot, low)
            return carry

        lax.fori_loop(first, last, step, 0)
        return (sums[0:count, :] / (closes - opens).astype(F32)).astype(BF)

    tokens = single.shape[0]
    half = tokens // 2
    for t in range(2):
        single[half * t : half * (t + 1), :] = block(table_col, half * t, half, col * tokens + half * t)
    width = row_terms.shape[1]
    count = 128
    for t in range(slab // count):
        term = dot(block(table_row, count * t, count, count * t), to_pair[:, :width])
        for u in range(count // 64):
            zz = t * (count // 64) + u
            row_terms[32 * zz : 32 * zz + 32, :] = jnp.where(
                core == 0, term[64 * u : 64 * u + 32], term[64 * u + 32 : 64 * u + 64]
            )
    all_terms = dot(single[...], to_pair[:, width:])
    sums[0:tokens, 0:width] = all_terms
    col_terms[...] = sums[pl.ds(pl.multiple_of(z * kz, 8), kz), 0:width]


def pair_kernel(groups, cols, halves, chunk_at, info, *refs):
    xs, refs = refs[:groups], refs[groups:]
    row_terms, col_terms, gain_in, gain_out, w_in, w_out, w_tri = refs[:7]
    outs, (left_buf, right_buf, rows_buf) = refs[7:-3], refs[-3:]
    k_first, valid, z, col = info[0], info[1], info[2], info[3]
    kb, per, channels = xs[0].shape
    lanes = per * groups
    for d in range(groups):
        zz = lax.rem(z - d + groups, groups)
        rows_buf[:, pl.ds(pl.multiple_of(zz * per, 32), per), :] = xs[d][...]
    at = k_first + chunk_at + pl.program_id(0) * kb
    tile = max(1, 1024 // lanes)
    repeat = tile * lanes // 128
    hidden = w_in.shape[0] // 2

    def opening(t):
        added = [
            (
                rows_buf[t + u].astype(F32) + row_terms[...] + col_terms[t + u : t + u + 1, :]
            ).astype(BF)
            for u in range(tile)
        ]
        paired = jnp.concatenate([value.astype(F32).T for value in added], axis=1)
        normed = normalize(paired, jnp.concatenate([gain_in[...]] * repeat, axis=1), 0).astype(BF)
        return paired, dot(w_in[...], normed)

    def closing(t, paired, gate_up):
        gate = 0.5 * gate_up[:hidden]
        inner = ((gate + gate * jnp.tanh(gate)) * gate_up[hidden:]).astype(BF)
        following = (paired + dot(w_out[...], inner)).astype(BF).astype(F32)
        normed = normalize(following, jnp.concatenate([gain_out[...]] * repeat, axis=1), 0).astype(BF)
        ops = dot(w_tri[...], normed)
        gate_l = jnp.tanh(0.5 * ops[:channels])
        gate_r = jnp.tanh(0.5 * ops[2 * channels : 3 * channels])
        val_l = ops[channels : 2 * channels]
        val_r = ops[3 * channels :]
        for u in range(tile):
            scale = jnp.where(at + t + u < valid, 0.5, 0.0).astype(F32)
            span = slice(lanes * u, lanes * (u + 1))
            left = val_l[:, span] * scale
            right = val_r[:, span] * scale
            left = left + left * gate_l[:, span]
            right = right + right * gate_r[:, span]
            for w in range(lanes // 128):
                part = slice(128 * w, 128 * (w + 1))
                left_buf[w, pl.ds(t + u, channels, stride=kb), :] = left[:, part]
                right_buf[w, pl.ds(t + u, channels, stride=kb), :] = right[:, part]

    ahead = opening(0)
    for t in range(0, kb, tile):
        held = ahead
        if t + tile < kb:
            ahead = opening(t + tile)
        closing(t, *held)
    each = channels // cols
    hc = each // 2
    for d in range(cols):
        for h in range(2):
            if halves == 2 and h == 1:
                out, at = outs[1 + d], (0, 0)
                first = (jnp.bitwise_xor(col, d) * each + hc) * kb
            else:
                out, at = outs[0], (d, h)
                first = (d * each + h * hc) * kb
            span = pl.ds(pl.multiple_of(first, 8), hc * kb)
            for w in range(lanes // 128):
                part = slice(128 * w, 128 * (w + 1))
                for side, buf in enumerate((left_buf, right_buf)):
                    piece = buf[w, span, :].reshape(hc, kb, 128)
                    out[at[0], at[1], side, :, :, part] = piece.astype(BF)


def triangle_kernel(groups, count, info, *refs):
    own, other = refs[:count], refs[count : -groups - 1]
    outs, buf = refs[-groups - 1 : -1], refs[-1]
    z = info[0]
    hc, lanes = own[0].shape[3], own[0].shape[5]
    for c in range(hc):
        left = jnp.concatenate([ref[d, 0, 0, c] for ref in own for d in range(ref.shape[0])], axis=0)
        for s, side in enumerate((own, other)):
            right = jnp.concatenate([ref[d, 0, 1, c] for ref in side for d in range(ref.shape[0])], axis=0)
            total = dot(left, right, TN)
            for w in range(lanes // 128):
                buf[s * (lanes // 128) + w, pl.ds(c, lanes, stride=hc), :] = total[
                    :, 128 * w : 128 * (w + 1)
                ]
    for d in range(groups):
        zz = lax.rem(z + d, groups)
        for w in range(2 * lanes // 128):
            piece = buf[w, pl.ds(pl.multiple_of(zz * 32 * hc, 32), 32 * hc), :]
            outs[d][:, :, 128 * w : 128 * (w + 1)] = piece.reshape(32, hc, 128).astype(BF)


def gather_kernel(groups, cols, *refs):
    parts, out = refs[:groups], refs[groups]
    total = parts[0][...].astype(F32)
    for d in range(1, groups):
        total = total + parts[d][...].astype(F32)
    half = total.shape[2] // 2
    split = total.shape[0] // 2
    for col in range(cols):
        pieces = [
            total[split * r : split * (r + 1), :, half * s + 32 * col : half * s + 32 * (col + 1)]
            for r in range(2)
            for s in range(2)
        ]
        out[col] = jnp.concatenate(pieces, axis=-1).astype(BF)


def finish_kernel(cols, info, first, second, gain, w_out, update):
    core = info[1]
    split = first.shape[1]
    for r in range(split):
        values = jnp.concatenate(
            [half[c, r].astype(F32) for c in range(cols) for half in (first, second)], axis=0
        )
        normed = normalize(values, gain[...], 0).astype(BF)
        rows = dot(normed, w_out[...], TN).astype(BF)
        for p in range(2):
            for s in range(2):
                at = pl.multiple_of((core if s == 0 else 1 - core) * 32, 32)
                update[split * p + r, pl.ds(at, 32), :] = rows[64 * p + 32 * s : 64 * p + 32 * s + 32]


def body(
    atom_feats,
    atom_bias,
    atom_counts,
    valid_tokens,
    pair_in,
    atom_gain,
    atom_proj,
    atom_out,
    atom_pool,
    single_to_pair,
    pair_gains,
    trans_in,
    trans_out,
    tri_in,
    tri_out,
):
    atom_rows, atom_width = atom_feats.shape
    rows_n, cols = lax.axis_size("row"), lax.axis_size("col")
    groups = rows_n // 2
    row, col = lax.axis_index("row"), lax.axis_index("col")
    z, core = row // 2, row % 2
    position = row * cols + col
    total_atoms = atom_rows * rows_n * cols
    tokens = atom_counts.shape[0]
    row_dev, tok_col, channels = pair_in.shape
    slab = row_dev * rows_n
    kz = tok_col // groups
    lanes = row_dev * groups
    each = channels // cols
    i32 = jnp.int32

    size = rows_n * cols
    up = [(i, i + 1) for i in range(size - 1)]
    down = [(j, i) for i, j in up]
    before = lax.ppermute(atom_feats[atom_rows - RIM :], ("row", "col"), up)
    after = lax.ppermute(atom_feats[:RIM], ("row", "col"), down)

    def shift_z(value, d):
        pairs = [(i, (i + 2 * d) % rows_n) for i in range(rows_n)]
        return lax.ppermute(value, "row", pairs)

    def cross_col(value, d):
        return lax.ppermute(value, "col", [(i, i ^ d) for i in range(cols)])

    def swap_core(value):
        return lax.ppermute(value, "row", [(i, i ^ 1) for i in range(rows_n)])

    unit = kz // 5
    chunks = ((0, 2), (2, 3))

    def spread_z(pieces):
        return [shift_z(piece, d) if d else piece for d, piece in enumerate(pieces)]

    def spread_col(value):
        return lax.all_to_all(value, "col", split_axis=0, concat_axis=0, tiled=True)

    def shares(z, first, steps):
        pieces = []
        for d in range(groups):
            start = ((z + d) % groups) * kz + first * unit
            piece = lax.dynamic_slice_in_dim(pair_in, start, steps * unit, 1)
            pieces.append(piece.transpose(1, 0, 2))
        return pieces

    pair_parts = [spread_z(shares(z, *chunks[0]))]

    heads = atom_bias.shape[0]
    updated = pl.pallas_call(
        functools.partial(atom_kernel, heads),
        out_shape=jax.ShapeDtypeStruct((atom_rows, atom_width), BF),
        in_specs=[SMEM] + [VMEM] * 7,
        out_specs=VMEM,
        scratch_shapes=[pltpu.VMEM((atom_rows + 2 * RIM, atom_width), BF)],
        compiler_params=params(),
        cost_estimate=cost(1e8, 1e6),
        name="atoms",
    )(
        jnp.stack([position * atom_rows, jnp.asarray(total_atoms, i32)]).astype(i32),
        before,
        atom_feats,
        after,
        atom_gain[None, :],
        atom_proj,
        atom_bias,
        atom_out,
    )

    updated, z_later, trans_in, trans_out, tri_in, gains = lax.optimization_barrier(
        (updated, z, trans_in, trans_out, tri_in, pair_gains)
    )
    plane = jnp.concatenate([updated] + [cross_col(updated, d) for d in range(1, cols)], axis=0)
    plane, pair_parts[0] = lax.optimization_barrier((plane, pair_parts[0]))
    planes = [plane] + [shift_z(plane, d) for d in range(1, groups)]
    later = [shares(z_later, *chunk) for chunk in chunks[1:]]
    weights = [
        jnp.broadcast_to(gains[0][:, None], (channels, 128)),
        jnp.broadcast_to(gains[1][:, None], (channels, 128)),
        trans_in.T,
        trans_out.T,
        tri_in.T,
    ]
    planes[1], later = lax.optimization_barrier((planes[1], later))
    planes, weights = lax.optimization_barrier((planes, weights))
    other = swap_core(jnp.concatenate(planes, axis=0))
    pair_parts += [spread_z(pieces) for pieces in later]

    ends = jnp.cumsum(atom_counts)
    starts = ends - atom_counts
    table = jnp.stack([starts, ends], axis=1)
    starts_all = jnp.concatenate([jnp.zeros((1,), i32), ends]).astype(i32)
    info = jnp.stack([z, core, col]).astype(i32)
    width = atom_pool.shape[1]
    padded_atoms = -(-total_atoms // CHUNK) * CHUNK + 32
    single, row_terms, col_terms = pl.pallas_call(
        functools.partial(pool_kernel, groups, cols, slab, kz),
        out_shape=(
            jax.ShapeDtypeStruct((tok_col, width), BF),
            jax.ShapeDtypeStruct((lanes, channels), F32),
            jax.ShapeDtypeStruct((kz, channels), F32),
        ),
        in_specs=[SMEM, SMEM] + [VMEM] * (groups + 5),
        out_specs=(VMEM, VMEM, VMEM),
        scratch_shapes=[
            pltpu.VMEM((padded_atoms, atom_width), BF),
            pltpu.VMEM((tok_col, width), F32),
        ],
        compiler_params=params(),
        cost_estimate=cost(1e3, 1e3),
        name="pool",
    )(
        info,
        starts_all,
        *planes,
        other,
        table[:slab],
        lax.dynamic_slice_in_dim(table, col * tok_col, tok_col),
        atom_pool,
        single_to_pair,
    )

    pair_info = jnp.stack([col * tok_col + z * kz, valid_tokens[0], z, col]).astype(i32)
    hc = each // 2
    operands = []

    def swap_joined(values):
        return swap_core(jnp.concatenate(values, axis=0) if len(values) > 1 else values[0])


    def exchange(values):
        operands.append([spread_col(values[0])])
        if len(values) > 1:
            got = [cross_col(value, d) if d else value for d, value in enumerate(values[1:])]
            operands.append(got)

    for call, (first, steps) in enumerate(chunks):
        halves = 2 if call == len(chunks) - 1 else 1
        inner = 2 // halves
        counts = [cols] + [1] * cols * (halves - 1)
        parts = pair_parts[call]
        if call:
            exchange(outs)
            _, parts = lax.optimization_barrier((outs, parts))
        whole = lambda *shape: pl.BlockSpec(shape, lambda g: (0,) * len(shape))
        outs = pl.pallas_call(
            functools.partial(pair_kernel, groups, cols, halves, first * unit),
            grid=(steps,),
            out_shape=[
                jax.ShapeDtypeStruct((blocks, inner, 2, hc, steps * unit, lanes), BF)
                for blocks in counts
            ],
            in_specs=[SMEM]
            + [pl.BlockSpec((unit, row_dev, channels), lambda g: (g, 0, 0))] * groups
            + [
                whole(lanes, channels),
                pl.BlockSpec((unit, channels), lambda g, first=first: (first + g, 0)),
                whole(channels, 128),
                whole(channels, 128),
                whole(*trans_in.shape[::-1]),
                whole(*trans_out.shape[::-1]),
                whole(4 * channels, channels),
            ],
            out_specs=[
                pl.BlockSpec((blocks, inner, 2, hc, unit, lanes), lambda g: (0, 0, 0, 0, g, 0))
                for blocks in counts
            ],
            scratch_shapes=[
                pltpu.VMEM((lanes // 128, channels * unit, 128), F32),
                pltpu.VMEM((lanes // 128, channels * unit, 128), F32),
                pltpu.VMEM((unit, lanes, channels), BF),
            ],
            compiler_params=params(),
            cost_estimate=cost(*((1e3, 1e3) if call == 0 else (3e10, 1e6))),
            name="pair",
        )(
            pair_info,
            *parts,
            row_terms,
            col_terms,
            *weights,
        )
    for at in range(len(operands)):
        operands[at], outs = lax.optimization_barrier((operands[at], outs))
        operands[at] = (operands[at], [swap_joined(operands[at])])
    exchange(outs)
    sent = None

    def finish_sum(parts):
        gathered = pl.pallas_call(
            functools.partial(gather_kernel, groups, cols),
            out_shape=jax.ShapeDtypeStruct((cols, row_dev // 2, hc, 128), BF),
            in_specs=[VMEM] * groups,
            out_specs=VMEM,
            compiler_params=params(),
            cost_estimate=cost(1e6, 3e6),
            name="gather",
        )(*parts)
        return spread_col(gathered)

    summed = []
    last = len(chunks) - 1
    for h in range(2):
        late = operands[last + h]
        if h:
            parts = spread_z(sent)
            late, parts[groups // 2] = lax.optimization_barrier((late, parts[groups // 2]))
            summed.append(finish_sum(parts))
        pairs = operands[:last] + [(late, [swap_joined(late)])]
        own, others = sum([p[0] for p in pairs], []), sum([p[1] for p in pairs], [])
        specs = [
            pl.BlockSpec(
                v.shape[:1] + (1,) + v.shape[2:],
                lambda g, at=h * (v.shape[1] - 1): (0, at, 0, 0, 0, 0),
            )
            for v in own + others
        ]
        sent = pl.pallas_call(
            functools.partial(triangle_kernel, groups, len(own)),
            grid=(1,),
            out_shape=[jax.ShapeDtypeStruct((row_dev, hc, 2 * lanes), BF)] * groups,
            in_specs=[SMEM] + specs,
            out_specs=[pl.BlockSpec((row_dev, hc, 2 * lanes), lambda g: (0, 0, 0))] * groups,
            scratch_shapes=[pltpu.VMEM((2 * lanes // 128, lanes * hc, 128), F32)],
            compiler_params=params(),
            cost_estimate=cost(4 * hc * lanes * lanes * tok_col, 1e7),
            name="triangle",
        )(info, *own, *others)
    summed.append(finish_sum(spread_z(sent)))
    update = pl.pallas_call(
        functools.partial(finish_kernel, cols),
        out_shape=jax.ShapeDtypeStruct((row_dev, slab // cols, channels), BF),
        in_specs=[SMEM] + [VMEM] * 4,
        out_specs=VMEM,
        compiler_params=params(),
        cost_estimate=cost(1e8, 1e6),
        name="finish",
    )(info, *summed, jnp.broadcast_to(gains[2][:, None], (channels, 128)), tri_out)
    return (single, update)


def solution(mesh):
    in_specs = (
        P(("row", "col"), None),
        P(None, ("row", "col"), None),
        P(),
        P(),
        P("row", "col", None),
        P(),
        P(),
        P(),
        P(),
        P(),
        P(),
        P(),
        P(),
        P(),
        P(),
    )
    out_specs = (P("col", None), P("row", "col", None))
    return jax.shard_map(body, mesh=mesh, in_specs=in_specs, out_specs=out_specs, check_vma=False)
```

```python
import functools

import jax
import jax.numpy as jnp
from jax import lax
from jax.experimental import pallas as pl
from jax.experimental.pallas import tpu as pltpu
from jax.sharding import PartitionSpec as P

QBLOCK = 32
KEYS = 128
RIM = 48
EPS = 1e-05
BF = jnp.bfloat16
F32 = jnp.float32

VMEM = pl.BlockSpec(memory_space=pltpu.VMEM)
SMEM = pl.BlockSpec(memory_space=pltpu.SMEM)
NT = (((1,), (1,)), ((), ()))
TN = (((0,), (0,)), ((), ()))


def params(limit=48):
    return pltpu.CompilerParams(vmem_limit_bytes=limit << 20)


def cost(flops, nbytes):
    return pl.CostEstimate(flops=int(flops), bytes_accessed=int(nbytes), transcendentals=0)


def dot(a, b, dims=(((1,), (0,)), ((), ()))):
    return lax.dot_general(a, b, dims, preferred_element_type=F32)


def normalize(values, gain, axis):
    average = jnp.mean(values, axis=axis, keepdims=True)
    centered = values - average
    variance = jnp.mean(centered * centered, axis=axis, keepdims=True)
    return centered * lax.rsqrt(variance + EPS) * gain


def atom_kernel(heads, info, before, own, after, gain, proj, bias, out_proj, out, feats):
    rows, width = own.shape
    first, total = info[0], info[1]
    feats[0:RIM, :] = before[...]
    feats[RIM : RIM + rows, :] = own[...]
    feats[RIM + rows :, :] = after[...]
    normed = normalize(feats[...].astype(F32), gain[...], -1).astype(BF)
    projected = dot(normed, proj[...])
    queries = projected[RIM : RIM + rows, :width].astype(BF)
    keys = projected[:, width : 2 * width].astype(BF)
    values = projected[:, 2 * width : 3 * width].astype(BF)
    gating = 0.5 + 0.5 * jnp.tanh(0.5 * projected[RIM : RIM + rows, 3 * width :])
    size = width // heads
    head_of = lax.broadcasted_iota(jnp.int32, (QBLOCK, width), 1) // size
    for b in range(rows // QBLOCK):
        lo = QBLOCK * b
        query = queries[lo : lo + QBLOCK].astype(F32)
        stacked = jnp.concatenate(
            [jnp.where(head_of == h, query, 0.0) for h in range(heads)], axis=0
        ).astype(BF)
        scores = dot(stacked, keys[lo : lo + KEYS], NT) * size ** (-0.5)
        scores = scores + jnp.concatenate([bias[h, lo : lo + QBLOCK, :] for h in range(heads)], axis=0)
        slot = lax.broadcasted_iota(jnp.int32, scores.shape, 1) + (first - RIM + lo)
        scores = jnp.where((slot >= 0) & (slot < total), scores, -1e30)
        exponent = jnp.exp(scores - jnp.max(scores, axis=-1, keepdims=True))
        weights = (exponent / jnp.sum(exponent, axis=-1, keepdims=True)).astype(BF)
        mixed = dot(weights, values[lo : lo + KEYS])
        blended = jnp.zeros((QBLOCK, width), F32)
        for h in range(heads):
            blended = jnp.where(head_of == h, mixed[QBLOCK * h : QBLOCK * (h + 1)], blended)
        gated = (blended * gating[lo : lo + QBLOCK]).astype(BF)
        own_rows = own[lo : lo + QBLOCK, :].astype(F32)
        out[lo : lo + QBLOCK, :] = (own_rows + dot(gated, out_proj[...])).astype(BF)


CHUNK = 512


def pool_kernel(
    groups, cols, slab, kz, info, starts, *refs
):
    parts, refs = refs[:groups], refs[groups:]
    other, table_row, table_col, pool, to_pair, single, row_terms, col_terms, atoms, sums = refs
    z, core, col = info[0], info[1], info[2]
    rows = parts[0].shape[0] // cols
    total = rows * cols * 2 * groups
    for d in range(groups):
        zz = lax.rem(z - d + groups, groups)
        for c in range(cols):
            for s in range(2):
                place = (zz * 2 + (core if s == 0 else 1 - core)) * cols + jnp.bitwise_xor(col, c)
                source = (
                    parts[d][rows * c : rows * (c + 1), :]
                    if s == 0
                    else other[rows * (d * cols + c) : rows * (d * cols + c + 1), :]
                )
                atoms[pl.ds(pl.multiple_of(place * rows, 32), rows), :] = source
    atoms[total:, :] = jnp.zeros((atoms.shape[0] - total, atoms.shape[1]), BF)

    def block(table, lo, count, first_token):
        begin = starts[first_token]
        finish = starts[first_token + count]
        opens = table[lo : lo + count, 0:1]
        closes = table[lo : lo + count, 1:2]
        first = lax.div(begin, CHUNK)
        last = lax.div(finish + CHUNK - 1, CHUNK)

        sums[0:count, :] = jnp.zeros((count, sums.shape[1]), F32)

        def step(i, carry):
            base = pl.multiple_of(i * CHUNK, CHUNK)
            hidden = jnp.maximum(dot(atoms[pl.ds(base, CHUNK), :], pool[...]), 0.0)
            high = hidden.astype(BF)
            low = (hidden - high.astype(F32)).astype(BF)
            place = lax.broadcasted_iota(jnp.int32, (count, CHUNK), 1) + base
            hot = jnp.where((place >= opens) & (place < closes), 1.0, 0.0).astype(BF)
            sums[0:count, :] += dot(
                jnp.concatenate([hot, hot], axis=1), jnp.concatenate([high, low], axis=0)
            )
            return carry

        lax.fori_loop(first, last, step, 0)
        return (sums[0:count, :] / (closes - opens).astype(F32)).astype(BF)

    tokens = single.shape[0]
    half = tokens // 2
    for t in range(2):
        single[half * t : half * (t + 1), :] = block(table_col, half * t, half, col * tokens + half * t)
    width = row_terms.shape[1]
    count = 128
    for t in range(slab // count):
        term = dot(block(table_row, count * t, count, count * t), to_pair[:, :width])
        for u in range(count // 64):
            zz = t * (count // 64) + u
            row_terms[32 * zz : 32 * zz + 32, :] = jnp.where(
                core == 0, term[64 * u : 64 * u + 32], term[64 * u + 32 : 64 * u + 64]
            )
    all_terms = dot(single[...], to_pair[:, width:])
    sums[0:tokens, 0:width] = all_terms
    col_terms[...] = sums[pl.ds(pl.multiple_of(z * kz, 8), kz), 0:width]


def pair_kernel(groups, cols, halves, chunk_at, info, *refs):
    xs, refs = refs[:groups], refs[groups:]
    row_terms, col_terms, gain_in, gain_out, w_in, w_out, w_tri = refs[:7]
    outs, (left_buf, right_buf, rows_buf) = refs[7:-3], refs[-3:]
    k_first, valid, z, col = info[0], info[1], info[2], info[3]
    kb, per, channels = xs[0].shape
    lanes = per * groups
    for d in range(groups):
        zz = lax.rem(z - d + groups, groups)
        rows_buf[:, pl.ds(pl.multiple_of(zz * per, 32), per), :] = xs[d][...]
    at = k_first + chunk_at + pl.program_id(0) * kb
    tile = max(1, 1024 // lanes)
    repeat = tile * lanes // 128
    hidden = w_in.shape[0] // 2

    def opening(t):
        added = [
            (
                rows_buf[t + u].astype(F32) + row_terms[...] + col_terms[t + u : t + u + 1, :]
            ).astype(BF)
            for u in range(tile)
        ]
        paired = jnp.concatenate([value.astype(F32).T for value in added], axis=1)
        normed = normalize(paired, jnp.concatenate([gain_in[...]] * repeat, axis=1), 0).astype(BF)
        return paired, dot(w_in[...], normed)

    def closing(t, paired, gate_up):
        gate = 0.5 * gate_up[:hidden]
        inner = ((gate + gate * jnp.tanh(gate)) * gate_up[hidden:]).astype(BF)
        following = (paired + dot(w_out[...], inner)).astype(BF).astype(F32)
        normed = normalize(following, jnp.concatenate([gain_out[...]] * repeat, axis=1), 0).astype(BF)
        ops = dot(w_tri[...], normed)
        gate_l = jnp.tanh(0.5 * ops[:channels])
        gate_r = jnp.tanh(0.5 * ops[2 * channels : 3 * channels])
        val_l = ops[channels : 2 * channels]
        val_r = ops[3 * channels :]
        for u in range(tile):
            scale = jnp.where(at + t + u < valid, 0.5, 0.0).astype(F32)
            span = slice(lanes * u, lanes * (u + 1))
            left = val_l[:, span] * scale
            right = val_r[:, span] * scale
            left = left + left * gate_l[:, span]
            right = right + right * gate_r[:, span]
            for w in range(lanes // 128):
                part = slice(128 * w, 128 * (w + 1))
                left_buf[w, pl.ds(t + u, channels, stride=kb), :] = left[:, part]
                right_buf[w, pl.ds(t + u, channels, stride=kb), :] = right[:, part]

    ahead = opening(0)
    for t in range(0, kb, tile):
        held = ahead
        if t + tile < kb:
            ahead = opening(t + tile)
        closing(t, *held)
    each = channels // cols
    hc = each // 2
    for d in range(cols):
        for h in range(2):
            if halves == 2 and h == 1:
                out, at = outs[1 + d], (0, 0)
                first = (jnp.bitwise_xor(col, d) * each + hc) * kb
            else:
                out, at = outs[0], (d, h)
                first = (d * each + h * hc) * kb
            span = pl.ds(pl.multiple_of(first, 8), hc * kb)
            for w in range(lanes // 128):
                part = slice(128 * w, 128 * (w + 1))
                for side, buf in enumerate((left_buf, right_buf)):
                    piece = buf[w, span, :].reshape(hc, kb, 128)
                    out[at[0], at[1], side, :, :, part] = piece.astype(BF)


def triangle_kernel(groups, count, info, *refs):
    own, other = refs[:count], refs[count : -groups - 1]
    outs, buf = refs[-groups - 1 : -1], refs[-1]
    z = info[0]
    hc, lanes = own[0].shape[3], own[0].shape[5]
    for c in range(hc):
        left = jnp.concatenate([ref[d, 0, 0, c] for ref in own for d in range(ref.shape[0])], axis=0)
        for s, side in enumerate((own, other)):
            right = jnp.concatenate([ref[d, 0, 1, c] for ref in side for d in range(ref.shape[0])], axis=0)
            total = dot(left, right, TN)
            for w in range(lanes // 128):
                buf[s * (lanes // 128) + w, pl.ds(c, lanes, stride=hc), :] = total[
                    :, 128 * w : 128 * (w + 1)
                ]
    for d in range(groups):
        zz = lax.rem(z + d, groups)
        for w in range(2 * lanes // 128):
            piece = buf[w, pl.ds(pl.multiple_of(zz * 32 * hc, 32), 32 * hc), :]
            outs[d][:, :, 128 * w : 128 * (w + 1)] = piece.reshape(32, hc, 128).astype(BF)


def gather_kernel(groups, cols, *refs):
    parts, out = refs[:groups], refs[groups]
    total = parts[0][...].astype(F32)
    for d in range(1, groups):
        total = total + parts[d][...].astype(F32)
    half = total.shape[2] // 2
    split = total.shape[0] // 2
    for col in range(cols):
        pieces = [
            total[split * r : split * (r + 1), :, half * s + 32 * col : half * s + 32 * (col + 1)]
            for r in range(2)
            for s in range(2)
        ]
        out[col] = jnp.concatenate(pieces, axis=-1).astype(BF)


def finish_kernel(cols, info, first, second, gain, w_out, update):
    core = info[1]
    split = first.shape[1]
    for r in range(split):
        values = jnp.concatenate(
            [half[c, r].astype(F32) for c in range(cols) for half in (first, second)], axis=0
        )
        normed = normalize(values, gain[...], 0).astype(BF)
        rows = dot(normed, w_out[...], TN).astype(BF)
        for p in range(2):
            for s in range(2):
                at = pl.multiple_of((core if s == 0 else 1 - core) * 32, 32)
                update[split * p + r, pl.ds(at, 32), :] = rows[64 * p + 32 * s : 64 * p + 32 * s + 32]


def body(
    atom_feats,
    atom_bias,
    atom_counts,
    valid_tokens,
    pair_in,
    atom_gain,
    atom_proj,
    atom_out,
    atom_pool,
    single_to_pair,
    pair_gains,
    trans_in,
    trans_out,
    tri_in,
    tri_out,
):
    atom_rows, atom_width = atom_feats.shape
    rows_n, cols = lax.axis_size("row"), lax.axis_size("col")
    groups = rows_n // 2
    row, col = lax.axis_index("row"), lax.axis_index("col")
    z, core = row // 2, row % 2
    position = row * cols + col
    total_atoms = atom_rows * rows_n * cols
    tokens = atom_counts.shape[0]
    row_dev, tok_col, channels = pair_in.shape
    slab = row_dev * rows_n
    kz = tok_col // groups
    lanes = row_dev * groups
    each = channels // cols
    i32 = jnp.int32

    size = rows_n * cols
    up = [(i, i + 1) for i in range(size - 1)]
    down = [(j, i) for i, j in up]
    before = lax.ppermute(atom_feats[atom_rows - RIM :], ("row", "col"), up)
    after = lax.ppermute(atom_feats[:RIM], ("row", "col"), down)

    def shift_z(value, d):
        pairs = [(i, (i + 2 * d) % rows_n) for i in range(rows_n)]
        return lax.ppermute(value, "row", pairs)

    def cross_col(value, d):
        return lax.ppermute(value, "col", [(i, i ^ d) for i in range(cols)])

    def swap_core(value):
        return lax.ppermute(value, "row", [(i, i ^ 1) for i in range(rows_n)])

    unit = kz // 5
    chunks = ((0, 2), (2, 3))

    def spread_z(pieces):
        return [shift_z(piece, d) if d else piece for d, piece in enumerate(pieces)]

    def spread_col(value):
        return lax.all_to_all(value, "col", split_axis=0, concat_axis=0, tiled=True)

    def shares(z, first, steps):
        pieces = []
        for d in range(groups):
            start = ((z + d) % groups) * kz + first * unit
            piece = lax.dynamic_slice_in_dim(pair_in, start, steps * unit, 1)
            pieces.append(piece.transpose(1, 0, 2))
        return pieces

    pair_parts = [spread_z(shares(z, *chunks[0]))]

    heads = atom_bias.shape[0]
    updated = pl.pallas_call(
        functools.partial(atom_kernel, heads),
        out_shape=jax.ShapeDtypeStruct((atom_rows, atom_width), BF),
        in_specs=[SMEM] + [VMEM] * 7,
        out_specs=VMEM,
        scratch_shapes=[pltpu.VMEM((atom_rows + 2 * RIM, atom_width), BF)],
        compiler_params=params(),
        cost_estimate=cost(1e8, 1e6),
        name="atoms",
    )(
        jnp.stack([position * atom_rows, jnp.asarray(total_atoms, i32)]).astype(i32),
        before,
        atom_feats,
        after,
        atom_gain[None, :],
        atom_proj,
        atom_bias,
        atom_out,
    )

    updated, z_later, trans_in, trans_out, tri_in, gains = lax.optimization_barrier(
        (updated, z, trans_in, trans_out, tri_in, pair_gains)
    )
    plane = jnp.concatenate([updated] + [cross_col(updated, d) for d in range(1, cols)], axis=0)
    plane, pair_parts[0] = lax.optimization_barrier((plane, pair_parts[0]))
    planes = [plane] + [shift_z(plane, d) for d in range(1, groups)]
    later = [shares(z_later, *chunk) for chunk in chunks[1:]]
    weights = [
        jnp.broadcast_to(gains[0][:, None], (channels, 128)),
        jnp.broadcast_to(gains[1][:, None], (channels, 128)),
        trans_in.T,
        trans_out.T,
        tri_in.T,
    ]
    planes[1], later = lax.optimization_barrier((planes[1], later))
    planes, weights = lax.optimization_barrier((planes, weights))
    other = swap_core(jnp.concatenate(planes, axis=0))
    pair_parts += [spread_z(pieces) for pieces in later]

    ends = jnp.cumsum(atom_counts)
    starts = ends - atom_counts
    table = jnp.stack([starts, ends], axis=1)
    starts_all = jnp.concatenate([jnp.zeros((1,), i32), ends]).astype(i32)
    info = jnp.stack([z, core, col]).astype(i32)
    width = atom_pool.shape[1]
    padded_atoms = -(-total_atoms // CHUNK) * CHUNK + 32
    single, row_terms, col_terms = pl.pallas_call(
        functools.partial(pool_kernel, groups, cols, slab, kz),
        out_shape=(
            jax.ShapeDtypeStruct((tok_col, width), BF),
            jax.ShapeDtypeStruct((lanes, channels), F32),
            jax.ShapeDtypeStruct((kz, channels), F32),
        ),
        in_specs=[SMEM, SMEM] + [VMEM] * (groups + 5),
        out_specs=(VMEM, VMEM, VMEM),
        scratch_shapes=[
            pltpu.VMEM((padded_atoms, atom_width), BF),
            pltpu.VMEM((tok_col, width), F32),
        ],
        compiler_params=params(),
        cost_estimate=cost(1e3, 1e3),
        name="pool",
    )(
        info,
        starts_all,
        *planes,
        other,
        table[:slab],
        lax.dynamic_slice_in_dim(table, col * tok_col, tok_col),
        atom_pool,
        single_to_pair,
    )

    row_terms = pltpu.with_memory_space_constraint(row_terms, pltpu.HBM)
    col_terms = pltpu.with_memory_space_constraint(col_terms, pltpu.HBM)
    pair_info = jnp.stack([col * tok_col + z * kz, valid_tokens[0], z, col]).astype(i32)
    hc = each // 2
    operands = []

    def swap_joined(values):
        return swap_core(jnp.concatenate(values, axis=0) if len(values) > 1 else values[0])


    def exchange(values):
        operands.append([spread_col(values[0])])
        if len(values) > 1:
            got = [cross_col(value, d) if d else value for d, value in enumerate(values[1:])]
            operands.append(got)

    for call, (first, steps) in enumerate(chunks):
        halves = 2 if call == len(chunks) - 1 else 1
        inner = 2 // halves
        counts = [cols] + [1] * cols * (halves - 1)
        parts = pair_parts[call]
        if call:
            exchange(outs)
            _, parts = lax.optimization_barrier((outs, parts))
        whole = lambda *shape: pl.BlockSpec(shape, lambda g: (0,) * len(shape))
        outs = pl.pallas_call(
            functools.partial(pair_kernel, groups, cols, halves, first * unit),
            grid=(steps,),
            out_shape=[
                jax.ShapeDtypeStruct((blocks, inner, 2, hc, steps * unit, lanes), BF)
                for blocks in counts
            ],
            in_specs=[SMEM]
            + [pl.BlockSpec((unit, row_dev, channels), lambda g: (g, 0, 0))] * groups
            + [
                whole(lanes, channels),
                pl.BlockSpec((unit, channels), lambda g, first=first: (first + g, 0)),
                whole(channels, 128),
                whole(channels, 128),
                whole(*trans_in.shape[::-1]),
                whole(*trans_out.shape[::-1]),
                whole(4 * channels, channels),
            ],
            out_specs=[
                pl.BlockSpec((blocks, inner, 2, hc, unit, lanes), lambda g: (0, 0, 0, 0, g, 0))
                for blocks in counts
            ],
            scratch_shapes=[
                pltpu.VMEM((lanes // 128, channels * unit, 128), F32),
                pltpu.VMEM((lanes // 128, channels * unit, 128), F32),
                pltpu.VMEM((unit, lanes, channels), BF),
            ],
            compiler_params=params(),
            cost_estimate=cost(*((1e3, 1e3) if call == 0 else (3e10, 1e6))),
            name="pair",
        )(
            pair_info,
            *parts,
            row_terms,
            col_terms,
            *weights,
        )
    for at in range(len(operands)):
        operands[at], outs = lax.optimization_barrier((operands[at], outs))
        operands[at] = (operands[at], [swap_joined(operands[at])])
    exchange(outs)
    sent = None

    def finish_sum(parts):
        gathered = pl.pallas_call(
            functools.partial(gather_kernel, groups, cols),
            out_shape=jax.ShapeDtypeStruct((cols, row_dev // 2, hc, 128), BF),
            in_specs=[VMEM] * groups,
            out_specs=VMEM,
            compiler_params=params(),
            cost_estimate=cost(1e6, 3e6),
            name="gather",
        )(*parts)
        return spread_col(gathered)

    summed = []
    last = len(chunks) - 1
    for h in range(2):
        late = operands[last + h]
        if h:
            parts = spread_z(sent)
            late, parts[groups // 2] = lax.optimization_barrier((late, parts[groups // 2]))
            summed.append(finish_sum(parts))
        pairs = operands[:last] + [(late, [swap_joined(late)])]
        own, others = sum([p[0] for p in pairs], []), sum([p[1] for p in pairs], [])
        specs = [
            pl.BlockSpec(
                v.shape[:1] + (1,) + v.shape[2:],
                lambda g, at=h * (v.shape[1] - 1): (0, at, 0, 0, 0, 0),
            )
            for v in own + others
        ]
        sent = pl.pallas_call(
            functools.partial(triangle_kernel, groups, len(own)),
            grid=(1,),
            out_shape=[jax.ShapeDtypeStruct((row_dev, hc, 2 * lanes), BF)] * groups,
            in_specs=[SMEM] + specs,
            out_specs=[pl.BlockSpec((row_dev, hc, 2 * lanes), lambda g: (0, 0, 0))] * groups,
            scratch_shapes=[pltpu.VMEM((2 * lanes // 128, lanes * hc, 128), F32)],
            compiler_params=params(),
            cost_estimate=cost(4 * hc * lanes * lanes * tok_col, 1e7),
            name="triangle",
        )(info, *own, *others)
    summed.append(finish_sum(spread_z(sent)))
    update = pl.pallas_call(
        functools.partial(finish_kernel, cols),
        out_shape=jax.ShapeDtypeStruct((row_dev, slab // cols, channels), BF),
        in_specs=[SMEM] + [VMEM] * 4,
        out_specs=VMEM,
        compiler_params=params(),
        cost_estimate=cost(1e8, 1e6),
        name="finish",
    )(info, *summed, jnp.broadcast_to(gains[2][:, None], (channels, 128)), tri_out)
    return (single, update)


def solution(mesh):
    in_specs = (
        P(("row", "col"), None),
        P(None, ("row", "col"), None),
        P(),
        P(),
        P("row", "col", None),
        P(),
        P(),
        P(),
        P(),
        P(),
        P(),
        P(),
        P(),
        P(),
        P(),
    )
    out_specs = (P("col", None), P("row", "col", None))
    return jax.shard_map(body, mesh=mesh, in_specs=in_specs, out_specs=out_specs, check_vma=False)
```

```python
import functools

import jax
import jax.numpy as jnp
from jax import lax
from jax.experimental import pallas as pl
from jax.experimental.pallas import tpu as pltpu
from jax.sharding import PartitionSpec as P

QBLOCK = 32
KEYS = 128
RIM = 48
EPS = 1e-05
BF = jnp.bfloat16
F32 = jnp.float32

VMEM = pl.BlockSpec(memory_space=pltpu.VMEM)
SMEM = pl.BlockSpec(memory_space=pltpu.SMEM)
NT = (((1,), (1,)), ((), ()))
TN = (((0,), (0,)), ((), ()))


def params(limit=48):
    return pltpu.CompilerParams(vmem_limit_bytes=limit << 20)


def cost(flops, nbytes):
    return pl.CostEstimate(flops=int(flops), bytes_accessed=int(nbytes), transcendentals=0)


def dot(a, b, dims=(((1,), (0,)), ((), ()))):
    return lax.dot_general(a, b, dims, preferred_element_type=F32)


def normalize(values, gain, axis):
    average = jnp.mean(values, axis=axis, keepdims=True)
    centered = values - average
    variance = jnp.mean(centered * centered, axis=axis, keepdims=True)
    return centered * lax.rsqrt(variance + EPS) * gain


def atom_kernel(heads, info, before, own, after, gain, proj, bias, out_proj, out, feats):
    rows, width = own.shape
    first, total = info[0], info[1]
    feats[0:RIM, :] = before[...]
    feats[RIM : RIM + rows, :] = own[...]
    feats[RIM + rows :, :] = after[...]
    normed = normalize(feats[...].astype(F32), gain[...], -1).astype(BF)
    projected = dot(normed, proj[...])
    queries = projected[RIM : RIM + rows, :width].astype(BF)
    keys = projected[:, width : 2 * width].astype(BF)
    values = projected[:, 2 * width : 3 * width].astype(BF)
    gating = 0.5 + 0.5 * jnp.tanh(0.5 * projected[RIM : RIM + rows, 3 * width :])
    size = width // heads
    head_of = lax.broadcasted_iota(jnp.int32, (QBLOCK, width), 1) // size
    for b in range(rows // QBLOCK):
        lo = QBLOCK * b
        query = queries[lo : lo + QBLOCK].astype(F32)
        stacked = jnp.concatenate(
            [jnp.where(head_of == h, query, 0.0) for h in range(heads)], axis=0
        ).astype(BF)
        scores = dot(stacked, keys[lo : lo + KEYS], NT) * size ** (-0.5)
        scores = scores + jnp.concatenate([bias[h, lo : lo + QBLOCK, :] for h in range(heads)], axis=0)
        slot = lax.broadcasted_iota(jnp.int32, scores.shape, 1) + (first - RIM + lo)
        scores = jnp.where((slot >= 0) & (slot < total), scores, -1e30)
        exponent = jnp.exp(scores - jnp.max(scores, axis=-1, keepdims=True))
        weights = (exponent / jnp.sum(exponent, axis=-1, keepdims=True)).astype(BF)
        mixed = dot(weights, values[lo : lo + KEYS])
        blended = jnp.zeros((QBLOCK, width), F32)
        for h in range(heads):
            blended = jnp.where(head_of == h, mixed[QBLOCK * h : QBLOCK * (h + 1)], blended)
        gated = (blended * gating[lo : lo + QBLOCK]).astype(BF)
        own_rows = own[lo : lo + QBLOCK, :].astype(F32)
        out[lo : lo + QBLOCK, :] = (own_rows + dot(gated, out_proj[...])).astype(BF)


CHUNK = 512


def pool_kernel(
    groups, cols, slab, kz, info, starts, *refs
):
    parts, refs = refs[:groups], refs[groups:]
    other, table_row, table_col, pool, to_pair, single, row_terms, col_terms, atoms, sums = refs
    z, core, col = info[0], info[1], info[2]
    rows = parts[0].shape[0] // cols
    total = rows * cols * 2 * groups
    for d in range(groups):
        zz = lax.rem(z - d + groups, groups)
        for c in range(cols):
            for s in range(2):
                place = (zz * 2 + (core if s == 0 else 1 - core)) * cols + jnp.bitwise_xor(col, c)
                source = (
                    parts[d][rows * c : rows * (c + 1), :]
                    if s == 0
                    else other[rows * (d * cols + c) : rows * (d * cols + c + 1), :]
                )
                atoms[pl.ds(pl.multiple_of(place * rows, 32), rows), :] = source
    atoms[total:, :] = jnp.zeros((atoms.shape[0] - total, atoms.shape[1]), BF)

    def block(table, lo, count, first_token):
        begin = starts[first_token]
        finish = starts[first_token + count]
        opens = table[lo : lo + count, 0:1]
        closes = table[lo : lo + count, 1:2]
        first = lax.div(begin, CHUNK)
        last = lax.div(finish + CHUNK - 1, CHUNK)

        sums[0:count, :] = jnp.zeros((count, sums.shape[1]), F32)

        def step(i, carry):
            base = pl.multiple_of(i * CHUNK, CHUNK)
            hidden = jnp.maximum(dot(atoms[pl.ds(base, CHUNK), :], pool[...]), 0.0)
            high = hidden.astype(BF)
            low = (hidden - high.astype(F32)).astype(BF)
            place = lax.broadcasted_iota(jnp.int32, (count, CHUNK), 1) + base
            hot = jnp.where((place >= opens) & (place < closes), 1.0, 0.0).astype(BF)
            sums[0:count, :] += dot(
                jnp.concatenate([hot, hot], axis=1), jnp.concatenate([high, low], axis=0)
            )
            return carry

        lax.fori_loop(first, last, step, 0)
        return (sums[0:count, :] / (closes - opens).astype(F32)).astype(BF)

    tokens = single.shape[0]
    half = tokens // 2
    for t in range(2):
        single[half * t : half * (t + 1), :] = block(table_col, half * t, half, col * tokens + half * t)
    width = row_terms.shape[1]
    count = 128
    for t in range(slab // count):
        term = dot(block(table_row, count * t, count, count * t), to_pair[:, :width])
        for u in range(count // 64):
            zz = t * (count // 64) + u
            row_terms[32 * zz : 32 * zz + 32, :] = jnp.where(
                core == 0, term[64 * u : 64 * u + 32], term[64 * u + 32 : 64 * u + 64]
            )
    all_terms = dot(single[...], to_pair[:, width:])
    sums[0:tokens, 0:width] = all_terms
    col_terms[...] = sums[pl.ds(pl.multiple_of(z * kz, 8), kz), 0:width]


def pair_kernel(groups, cols, halves, chunk_at, info, *refs):
    xs, refs = refs[:groups], refs[groups:]
    row_terms, col_terms, gain_in, gain_out, w_in, w_out, w_tri = refs[:7]
    outs, (left_buf, right_buf, rows_buf) = refs[7:-3], refs[-3:]
    k_first, valid, z, col = info[0], info[1], info[2], info[3]
    kb, per, channels = xs[0].shape
    lanes = per * groups
    for d in range(groups):
        zz = lax.rem(z - d + groups, groups)
        rows_buf[:, pl.ds(pl.multiple_of(zz * per, 32), per), :] = xs[d][...]
    at = k_first + chunk_at + pl.program_id(0) * kb
    tile = min(kb, max(1, 2048 // lanes))
    repeat = tile * lanes // 128
    hidden = w_in.shape[0] // 2

    def opening(t):
        added = [
            (
                rows_buf[t + u].astype(F32) + row_terms[...] + col_terms[t + u : t + u + 1, :]
            ).astype(BF)
            for u in range(tile)
        ]
        paired = jnp.concatenate([value.astype(F32).T for value in added], axis=1)
        normed = normalize(paired, jnp.concatenate([gain_in[...]] * repeat, axis=1), 0).astype(BF)
        return paired, dot(w_in[...], normed)

    def closing(t, paired, gate_up):
        gate = 0.5 * gate_up[:hidden]
        inner = ((gate + gate * jnp.tanh(gate)) * gate_up[hidden:]).astype(BF)
        following = (paired + dot(w_out[...], inner)).astype(BF).astype(F32)
        normed = normalize(following, jnp.concatenate([gain_out[...]] * repeat, axis=1), 0).astype(BF)
        ops = dot(w_tri[...], normed)
        gate_l = jnp.tanh(0.5 * ops[:channels])
        gate_r = jnp.tanh(0.5 * ops[2 * channels : 3 * channels])
        val_l = ops[channels : 2 * channels]
        val_r = ops[3 * channels :]
        for u in range(tile):
            scale = jnp.where(at + t + u < valid, 0.5, 0.0).astype(F32)
            span = slice(lanes * u, lanes * (u + 1))
            left = val_l[:, span] * scale
            right = val_r[:, span] * scale
            left = left + left * gate_l[:, span]
            right = right + right * gate_r[:, span]
            for w in range(lanes // 128):
                part = slice(128 * w, 128 * (w + 1))
                left_buf[w, pl.ds(t + u, channels, stride=kb), :] = left[:, part]
                right_buf[w, pl.ds(t + u, channels, stride=kb), :] = right[:, part]

    ahead = opening(0)
    for t in range(0, kb, tile):
        held = ahead
        if t + tile < kb:
            ahead = opening(t + tile)
        closing(t, *held)
    each = channels // cols
    hc = each // 2
    for d in range(cols):
        for h in range(2):
            if halves == 2 and h == 1:
                out, at = outs[1 + d], (0, 0)
                first = (jnp.bitwise_xor(col, d) * each + hc) * kb
            else:
                out, at = outs[0], (d, h)
                first = (d * each + h * hc) * kb
            span = pl.ds(pl.multiple_of(first, 8), hc * kb)
            for w in range(lanes // 128):
                part = slice(128 * w, 128 * (w + 1))
                for side, buf in enumerate((left_buf, right_buf)):
                    piece = buf[w, span, :].reshape(hc, kb, 128)
                    out[at[0], at[1], side, :, :, part] = piece.astype(BF)


def triangle_kernel(groups, count, info, *refs):
    own, other = refs[:count], refs[count : -groups - 1]
    outs, buf = refs[-groups - 1 : -1], refs[-1]
    z = info[0]
    hc, lanes = own[0].shape[3], own[0].shape[5]
    for c in range(hc):
        left = jnp.concatenate([ref[d, 0, 0, c] for ref in own for d in range(ref.shape[0])], axis=0)
        for s, side in enumerate((own, other)):
            right = jnp.concatenate([ref[d, 0, 1, c] for ref in side for d in range(ref.shape[0])], axis=0)
            total = dot(left, right, TN)
            for w in range(lanes // 128):
                buf[s * (lanes // 128) + w, pl.ds(c, lanes, stride=hc), :] = total[
                    :, 128 * w : 128 * (w + 1)
                ]
    for d in range(groups):
        zz = lax.rem(z + d, groups)
        for w in range(2 * lanes // 128):
            piece = buf[w, pl.ds(pl.multiple_of(zz * 32 * hc, 32), 32 * hc), :]
            outs[d][:, :, 128 * w : 128 * (w + 1)] = piece.reshape(32, hc, 128).astype(BF)


def gather_kernel(groups, cols, *refs):
    parts, out = refs[:groups], refs[groups]
    total = parts[0][...].astype(F32)
    for d in range(1, groups):
        total = total + parts[d][...].astype(F32)
    half = total.shape[2] // 2
    split = total.shape[0] // 2
    for col in range(cols):
        pieces = [
            total[split * r : split * (r + 1), :, half * s + 32 * col : half * s + 32 * (col + 1)]
            for r in range(2)
            for s in range(2)
        ]
        out[col] = jnp.concatenate(pieces, axis=-1).astype(BF)


def finish_kernel(cols, info, first, second, gain, w_out, update):
    core = info[1]
    split = first.shape[1]
    for r in range(split):
        values = jnp.concatenate(
            [half[c, r].astype(F32) for c in range(cols) for half in (first, second)], axis=0
        )
        normed = normalize(values, gain[...], 0).astype(BF)
        rows = dot(normed, w_out[...], TN).astype(BF)
        for p in range(2):
            for s in range(2):
                at = pl.multiple_of((core if s == 0 else 1 - core) * 32, 32)
                update[split * p + r, pl.ds(at, 32), :] = rows[64 * p + 32 * s : 64 * p + 32 * s + 32]


def body(
    atom_feats,
    atom_bias,
    atom_counts,
    valid_tokens,
    pair_in,
    atom_gain,
    atom_proj,
    atom_out,
    atom_pool,
    single_to_pair,
    pair_gains,
    trans_in,
    trans_out,
    tri_in,
    tri_out,
):
    atom_rows, atom_width = atom_feats.shape
    rows_n, cols = lax.axis_size("row"), lax.axis_size("col")
    groups = rows_n // 2
    row, col = lax.axis_index("row"), lax.axis_index("col")
    z, core = row // 2, row % 2
    position = row * cols + col
    total_atoms = atom_rows * rows_n * cols
    tokens = atom_counts.shape[0]
    row_dev, tok_col, channels = pair_in.shape
    slab = row_dev * rows_n
    kz = tok_col // groups
    lanes = row_dev * groups
    each = channels // cols
    i32 = jnp.int32

    size = rows_n * cols
    up = [(i, i + 1) for i in range(size - 1)]
    down = [(j, i) for i, j in up]
    before = lax.ppermute(atom_feats[atom_rows - RIM :], ("row", "col"), up)
    after = lax.ppermute(atom_feats[:RIM], ("row", "col"), down)

    def shift_z(value, d):
        pairs = [(i, (i + 2 * d) % rows_n) for i in range(rows_n)]
        return lax.ppermute(value, "row", pairs)

    def cross_col(value, d):
        return lax.ppermute(value, "col", [(i, i ^ d) for i in range(cols)])

    def swap_core(value):
        return lax.ppermute(value, "row", [(i, i ^ 1) for i in range(rows_n)])

    unit = kz // 5
    chunks = ((0, 2), (2, 3))

    def spread_z(pieces):
        return [shift_z(piece, d) if d else piece for d, piece in enumerate(pieces)]

    def spread_col(value):
        return lax.all_to_all(value, "col", split_axis=0, concat_axis=0, tiled=True)

    def shares(z, first, steps):
        pieces = []
        for d in range(groups):
            start = ((z + d) % groups) * kz + first * unit
            piece = lax.dynamic_slice_in_dim(pair_in, start, steps * unit, 1)
            pieces.append(piece.transpose(1, 0, 2))
        return pieces

    pair_parts = [spread_z(shares(z, *chunks[0]))]

    heads = atom_bias.shape[0]
    updated = pl.pallas_call(
        functools.partial(atom_kernel, heads),
        out_shape=jax.ShapeDtypeStruct((atom_rows, atom_width), BF),
        in_specs=[SMEM] + [VMEM] * 7,
        out_specs=VMEM,
        scratch_shapes=[pltpu.VMEM((atom_rows + 2 * RIM, atom_width), BF)],
        compiler_params=params(),
        cost_estimate=cost(1e8, 1e6),
        name="atoms",
    )(
        jnp.stack([position * atom_rows, jnp.asarray(total_atoms, i32)]).astype(i32),
        before,
        atom_feats,
        after,
        atom_gain[None, :],
        atom_proj,
        atom_bias,
        atom_out,
    )

    updated, z_later, trans_in, trans_out, tri_in, gains = lax.optimization_barrier(
        (updated, z, trans_in, trans_out, tri_in, pair_gains)
    )
    plane = jnp.concatenate([updated] + [cross_col(updated, d) for d in range(1, cols)], axis=0)
    plane, pair_parts[0] = lax.optimization_barrier((plane, pair_parts[0]))
    planes = [plane] + [shift_z(plane, d) for d in range(1, groups)]
    later = [shares(z_later, *chunk) for chunk in chunks[1:]]
    weights = [
        jnp.broadcast_to(gains[0][:, None], (channels, 128)),
        jnp.broadcast_to(gains[1][:, None], (channels, 128)),
        trans_in.T,
        trans_out.T,
        tri_in.T,
    ]
    planes[1], later = lax.optimization_barrier((planes[1], later))
    planes, weights = lax.optimization_barrier((planes, weights))
    other = swap_core(jnp.concatenate(planes, axis=0))
    pair_parts += [spread_z(pieces) for pieces in later]

    ends = jnp.cumsum(atom_counts)
    starts = ends - atom_counts
    table = jnp.stack([starts, ends], axis=1)
    starts_all = jnp.concatenate([jnp.zeros((1,), i32), ends]).astype(i32)
    info = jnp.stack([z, core, col]).astype(i32)
    width = atom_pool.shape[1]
    padded_atoms = -(-total_atoms // CHUNK) * CHUNK + 32
    single, row_terms, col_terms = pl.pallas_call(
        functools.partial(pool_kernel, groups, cols, slab, kz),
        out_shape=(
            jax.ShapeDtypeStruct((tok_col, width), BF),
            jax.ShapeDtypeStruct((lanes, channels), F32),
            jax.ShapeDtypeStruct((kz, channels), F32),
        ),
        in_specs=[SMEM, SMEM] + [VMEM] * (groups + 5),
        out_specs=(VMEM, VMEM, VMEM),
        scratch_shapes=[
            pltpu.VMEM((padded_atoms, atom_width), BF),
            pltpu.VMEM((tok_col, width), F32),
        ],
        compiler_params=params(),
        cost_estimate=cost(1e3, 1e3),
        name="pool",
    )(
        info,
        starts_all,
        *planes,
        other,
        table[:slab],
        lax.dynamic_slice_in_dim(table, col * tok_col, tok_col),
        atom_pool,
        single_to_pair,
    )

    row_terms = pltpu.with_memory_space_constraint(row_terms, pltpu.HBM)
    col_terms = pltpu.with_memory_space_constraint(col_terms, pltpu.HBM)
    pair_info = jnp.stack([col * tok_col + z * kz, valid_tokens[0], z, col]).astype(i32)
    hc = each // 2
    operands = []

    def swap_joined(values):
        return swap_core(jnp.concatenate(values, axis=0) if len(values) > 1 else values[0])


    def exchange(values):
        operands.append([spread_col(values[0])])
        if len(values) > 1:
            got = [cross_col(value, d) if d else value for d, value in enumerate(values[1:])]
            operands.append(got)

    for call, (first, steps) in enumerate(chunks):
        halves = 2 if call == len(chunks) - 1 else 1
        inner = 2 // halves
        counts = [cols] + [1] * cols * (halves - 1)
        parts = pair_parts[call]
        if call:
            exchange(outs)
            _, parts = lax.optimization_barrier((outs, parts))
        whole = lambda *shape: pl.BlockSpec(shape, lambda g: (0,) * len(shape))
        outs = pl.pallas_call(
            functools.partial(pair_kernel, groups, cols, halves, first * unit),
            grid=(steps,),
            out_shape=[
                jax.ShapeDtypeStruct((blocks, inner, 2, hc, steps * unit, lanes), BF)
                for blocks in counts
            ],
            in_specs=[SMEM]
            + [pl.BlockSpec((unit, row_dev, channels), lambda g: (g, 0, 0))] * groups
            + [
                whole(lanes, channels),
                pl.BlockSpec((unit, channels), lambda g, first=first: (first + g, 0)),
                whole(channels, 128),
                whole(channels, 128),
                whole(*trans_in.shape[::-1]),
                whole(*trans_out.shape[::-1]),
                whole(4 * channels, channels),
            ],
            out_specs=[
                pl.BlockSpec((blocks, inner, 2, hc, unit, lanes), lambda g: (0, 0, 0, 0, g, 0))
                for blocks in counts
            ],
            scratch_shapes=[
                pltpu.VMEM((lanes // 128, channels * unit, 128), F32),
                pltpu.VMEM((lanes // 128, channels * unit, 128), F32),
                pltpu.VMEM((unit, lanes, channels), BF),
            ],
            compiler_params=params(),
            cost_estimate=cost(*((1e3, 1e3) if call == 0 else (3e10, 1e6))),
            name="pair",
        )(
            pair_info,
            *parts,
            row_terms,
            col_terms,
            *weights,
        )
    for at in range(len(operands)):
        operands[at], outs = lax.optimization_barrier((operands[at], outs))
        operands[at] = (operands[at], [swap_joined(operands[at])])
    exchange(outs)
    sent = None

    def finish_sum(parts):
        gathered = pl.pallas_call(
            functools.partial(gather_kernel, groups, cols),
            out_shape=jax.ShapeDtypeStruct((cols, row_dev // 2, hc, 128), BF),
            in_specs=[VMEM] * groups,
            out_specs=VMEM,
            compiler_params=params(),
            cost_estimate=cost(1e6, 3e6),
            name="gather",
        )(*parts)
        return spread_col(gathered)

    summed = []
    last = len(chunks) - 1
    for h in range(2):
        late = operands[last + h]
        if h:
            parts = spread_z(sent)
            late, parts[groups // 2] = lax.optimization_barrier((late, parts[groups // 2]))
            summed.append(finish_sum(parts))
        pairs = operands[:last] + [(late, [swap_joined(late)])]
        own, others = sum([p[0] for p in pairs], []), sum([p[1] for p in pairs], [])
        specs = [
            pl.BlockSpec(
                v.shape[:1] + (1,) + v.shape[2:],
                lambda g, at=h * (v.shape[1] - 1): (0, at, 0, 0, 0, 0),
            )
            for v in own + others
        ]
        sent = pl.pallas_call(
            functools.partial(triangle_kernel, groups, len(own)),
            grid=(1,),
            out_shape=[jax.ShapeDtypeStruct((row_dev, hc, 2 * lanes), BF)] * groups,
            in_specs=[SMEM] + specs,
            out_specs=[pl.BlockSpec((row_dev, hc, 2 * lanes), lambda g: (0, 0, 0))] * groups,
            scratch_shapes=[pltpu.VMEM((2 * lanes // 128, lanes * hc, 128), F32)],
            compiler_params=params(),
            cost_estimate=cost(4 * hc * lanes * lanes * tok_col, 1e7),
            name="triangle",
        )(info, *own, *others)
    summed.append(finish_sum(spread_z(sent)))
    update = pl.pallas_call(
        functools.partial(finish_kernel, cols),
        out_shape=jax.ShapeDtypeStruct((row_dev, slab // cols, channels), BF),
        in_specs=[SMEM] + [VMEM] * 4,
        out_specs=VMEM,
        compiler_params=params(),
        cost_estimate=cost(1e8, 1e6),
        name="finish",
    )(info, *summed, jnp.broadcast_to(gains[2][:, None], (channels, 128)), tri_out)
    return (single, update)


def solution(mesh):
    in_specs = (
        P(("row", "col"), None),
        P(None, ("row", "col"), None),
        P(),
        P(),
        P("row", "col", None),
        P(),
        P(),
        P(),
        P(),
        P(),
        P(),
        P(),
        P(),
        P(),
        P(),
    )
    out_specs = (P("col", None), P("row", "col", None))
    return jax.shard_map(body, mesh=mesh, in_specs=in_specs, out_specs=out_specs, check_vma=False)
```
